256 devices in a mesh: grp: 4 (over y), wide: 64 (over z, x, core).
Axes of the slice: x: 4, y: 4, z: 8, core: 2. Of those that a mesh axis runs over, the one named last changes fastest.
Arguments:
- coeff: float32 [2048, 6144], P(('grp', 'wide')), may hold values from -6 to 6
- beta_blocks: float32 [96, 128, 128], replicated, may hold values from -0.5 to 0.5
- block_list: int32 [2, 96], replicated, may hold values from 0 to 47
- alpha_blocks: float32 [256, 4, 8, 8], P(('grp', 'wide')), may hold values from -2 to 2
- partner_mask: int32 [256, 4], P(('grp', 'wide')), may hold values 0 or 1
- exc_source: int32 [90, 2048], P(None, 'grp'), may hold values from 0 to 2047
- exc_pair: int32 [90, 2048], P(None, 'grp'), may hold values from 0 to 323
- exc_parity: int32 [90, 2048], P(None, 'grp'), may hold values from 0 to 1
- occupation: int32 [18, 6144], P(None, 'wide'), may hold values 0 or 1
- coulomb: float32 [324, 18], replicated, may hold values from -0.2 to 0.2
Outputs:
- sigma: float32 [2048, 6144], P(('grp', 'wide'))
The draws below stay inside these ranges and needn't reach their ends.
Inputs may be any that keep to these rules, and one draw needn't show every extreme that they name: `exc_source`: any alpha string.
All inputs are finite; a program needn't handle non-finite values. No bound on the sum of `partner_mask` or of `occupation` on one device may be relied on, other than what follows from the above.
Results may differ from the reference program's by a relative error of at most 0.0003.
Values sent between devices are 32-bit elements; how exact they have to be, the bound alone decides.
No kernel may reach another device: no remote copies, remote signals or barrier semaphores. Data moves between devices by JAX's collectives and lax.ppermute only.
A program may use at most 128 MiB of HBM per device.

```python
import jax
import jax.numpy as jnp
from jax import lax

RA = 8
NB = 6144
SB = 128
P_SIZE = 96
NORB = 18
NEXC = 90
NPAIR = 324
NBB = 48
ABLK = 256
NA = 2048
N_GRP = 4
N_WIDE = 64


def place_ends(result, stream_key, least, top_value):
    dims = result.shape
    place = [jax.random.randint(jax.random.fold_in(stream_key, axis), (), 0, dims[axis]) for axis in range(len(dims))]
    result = result.at[tuple(place)].set(least)
    longest = dims.index(max(dims))
    place[longest] = (place[longest] + 1) % dims[longest]
    return result.at[tuple(place)].set(top_value)


def block_levels(key, dims, shards, smallest, top_value):
    level = 1.0
    for dim, blocks in shards:
        draws = jax.random.uniform(jax.random.fold_in(jax.random.fold_in(key, 6), dim), (blocks,), jnp.float32, smallest / len(shards), top_value / len(shards))
        level = level * jnp.repeat(jnp.exp(draws), dims[dim] // blocks).reshape((-1,) + (1,) * (len(dims) - 1 - dim))
    return level


def bell_draw(stream_key, shape, deviation, limit, cuts=(), dtype=jnp.bfloat16):
    result = jax.random.normal(stream_key, shape, jnp.float32) * deviation
    if len(cuts) > 0:
        result = block_levels(stream_key, shape, cuts, -0.22, 0.18) * result
    return jnp.clip(result, min=-limit, max=limit).astype(dtype)


def setup_inputs(seed: int = 0) -> dict:
    keys = jax.random.split(jax.random.key(seed), 11)
    coeff = bell_draw(keys[0], (NA, NB), 1.0, 6.0, ((0, 256),), jnp.float32)
    beta_blocks = bell_draw(keys[1], (P_SIZE, SB, SB), SB ** -0.5, 0.5, (), jnp.float32)
    block_list = place_ends(jax.random.randint(keys[2], (2, P_SIZE), 0, NBB), jax.random.fold_in(keys[2], 1), 0, NBB - 1).astype(jnp.int32)
    alpha_blocks = bell_draw(keys[3], (ABLK, N_GRP, RA, RA), RA ** -0.5, 2.0, ((0, 256),), jnp.float32)
    partner_mask = place_ends((jax.random.randint(keys[4], (ABLK, N_GRP), 0, 3) < 2).astype(jnp.int32), jax.random.fold_in(keys[4], 1), 0, 1)
    exc_source = place_ends(jax.random.randint(keys[5], (NEXC, NA), 0, NA), jax.random.fold_in(keys[5], 1), 0, NA - 1).astype(jnp.int32)
    exc_pair = place_ends(jax.random.randint(keys[6], (NEXC, NA), 0, NPAIR), jax.random.fold_in(keys[6], 1), 0, NPAIR - 1).astype(jnp.int32)
    exc_parity = place_ends(jax.random.randint(keys[7], (NEXC, NA), 0, 2), jax.random.fold_in(keys[7], 1), 0, 1).astype(jnp.int32)
    occupation = place_ends((jax.random.randint(keys[8], (NORB, NB), 0, 2) < 1).astype(jnp.int32), jax.random.fold_in(keys[8], 1), 0, 1)
    coulomb = bell_draw(keys[9], (NPAIR, NORB), 0.035, 0.2, (), jnp.float32)
    return {"coeff": coeff, "beta_blocks": beta_blocks, "block_list": block_list, "alpha_blocks": alpha_blocks, "partner_mask": partner_mask, "exc_source": exc_source, "exc_pair": exc_pair, "exc_parity": exc_parity, "occupation": occupation, "coulomb": coulomb}


HIGH = lax.Precision.HIGHEST


def reference(coeff, beta_blocks, block_list, alpha_blocks, partner_mask, exc_source, exc_pair, exc_parity, occupation, coulomb):
    blocked = coeff.reshape(NA, NBB, SB)

    def add_block(index, accum):
        source = block_list[0, index].astype(jnp.int32)
        target = block_list[1, index].astype(jnp.int32)
        column = lax.dynamic_index_in_dim(blocked, source, 1, keepdims=False)
        term = jnp.dot(column, beta_blocks[index], precision=HIGH, preferred_element_type=jnp.float32)
        before = lax.dynamic_index_in_dim(accum, target, 1, keepdims=False)
        return lax.dynamic_update_index_in_dim(accum, before + term, target, 1)

    same_beta = lax.fori_loop(0, P_SIZE, add_block, jnp.zeros((NA, NBB, SB), jnp.float32)).reshape(NA, NB)

    grouped = coeff.reshape(N_GRP, N_WIDE, RA, NB)
    masked = alpha_blocks.reshape(N_GRP, N_WIDE, N_GRP, RA, RA) * partner_mask.reshape(N_GRP, N_WIDE, N_GRP)[:, :, :, None, None].astype(jnp.float32)
    same_alpha = jnp.einsum("gwhrs,hwsn->gwrn", masked, grouped, precision=HIGH).reshape(NA, NB)

    weights = jnp.dot(coulomb, occupation.astype(jnp.float32), precision=HIGH, preferred_element_type=jnp.float32)

    def add_single(accum, entry):
        source, pair_row, parity = entry
        fetched = jnp.take(coeff, source.astype(jnp.int32), axis=0)
        factor = jnp.take(weights, pair_row.astype(jnp.int32), axis=0)
        phase = 1.0 - 2.0 * parity.astype(jnp.float32)
        return accum + phase[:, None] * factor * fetched, None

    mixed, _ = lax.scan(add_single, jnp.zeros((NA, NB), jnp.float32), (exc_source, exc_pair, exc_parity))
    return same_beta + same_alpha + mixed
```

```python
import functools

import jax
import jax.numpy as jnp
from jax import lax
from jax.experimental import pallas as pl
from jax.experimental.pallas import tpu as pltpu
from jax.sharding import Mesh
from jax.sharding import PartitionSpec as P

HIGH = lax.Precision.HIGHEST
RA = 8
LANES = 128
N_GRP = 4
NZ, NX, NC = 8, 4, 2
NQ = NZ * NX
COLS = 192
PAD = 8

SMEM = pl.BlockSpec(memory_space=pltpu.SMEM)
VMEM = pl.BlockSpec(memory_space=pltpu.VMEM)
ANY = pl.BlockSpec(memory_space=pl.ANY)


def pack_kernel(x_ref, o_ref):
    zeros = jnp.zeros((RA, LANES - COLS + LANES), jnp.float32)
    for j in range(NQ):
        o_ref[j, 0] = x_ref[:, COLS * j : COLS * j + LANES]
        o_ref[j, 1] = jnp.concatenate(
            [x_ref[:, COLS * j + LANES : COLS * (j + 1)], zeros], axis=1
        )


def pack(coeff):
    return pl.pallas_call(
        pack_kernel,
        out_shape=jax.ShapeDtypeStruct((NQ, 2, RA, LANES), jnp.float32),
        in_specs=[VMEM],
        out_specs=VMEM,
        name="pack",
    )(coeff)


def mixed_kernel(n_exc, row_count, c_ref, cidx_ref, widx_ref, w_ref, *rest):
    parts = rest[: 2 * N_GRP]
    o_ref, table, sem = rest[2 * N_GRP :]
    part_rows = NQ * 2 * RA
    copies = []
    for i, part in enumerate(parts):
        copy = pltpu.make_async_copy(
            part, table.at[pl.ds(i * part_rows, part_rows)], sem.at[i]
        )
        copy.start()
        copies.append(copy)
    for copy in copies:
        copy.wait()
    core = c_ref[0]
    span = row_count - 2 * RA + 1

    def block(q, carry):
        start = q * (2 * RA) + core * RA
        for a in range(RA):
            acc = None
            for e in range(n_exc):
                base = e * row_count + a
                ci = cidx_ref.at[pl.ds(base, span + RA)][start]
                wi = widx_ref.at[pl.ds(base, span + RA)][start]
                term = (
                    table[pl.ds(ci, 2, stride=RA), :]
                    * w_ref[pl.ds(wi, 2, stride=RA), :]
                )
                acc = term if acc is None else acc + term
            o_ref[pl.ds(q * (2 * RA) + a, 2, stride=RA), :] = acc
        return carry

    lax.fori_loop(0, NQ, block, 0)


def mixed_call(core, cidx, widx, wtab, parts, n_exc, row_count):
    part_rows = NQ * 2 * RA
    return pl.pallas_call(
        functools.partial(mixed_kernel, n_exc, row_count),
        out_shape=jax.ShapeDtypeStruct((part_rows, LANES), jnp.float32),
        in_specs=[SMEM, SMEM, SMEM, VMEM] + [ANY] * len(parts),
        out_specs=VMEM,
        scratch_shapes=[
            pltpu.VMEM((2 * N_GRP * part_rows, LANES), jnp.float32),
            pltpu.SemaphoreType.DMA((2 * N_GRP,)),
        ],
        compiler_params=pltpu.CompilerParams(vmem_limit_bytes=32 << 20),
        cost_estimate=pl.CostEstimate(
            flops=2 * n_exc * row_count * COLS // 2,
            bytes_accessed=8 << 20,
            transcendentals=0,
        ),
        name="mixed",
    )(core, cidx, widx, wtab, *parts)


def final_kernel(m_ref, b_ref, k_ref, x0, x1, x2, x3, o_ref):
    k = k_ref[...]
    xs = (x0, x1, x2, x3)
    for j in range(NQ):
        lo = COLS * j
        a = m_ref[j, 0]
        b = m_ref[j, 1][:, : COLS - LANES]
        o_ref[:, lo : lo + COLS] = jnp.concatenate([a, b], axis=1)
    width = 1024
    for t in range(b_ref.shape[1] // width):
        cols = slice(t * width, (t + 1) * width)
        stacked = jnp.concatenate([x[:, cols] for x in xs], axis=0)
        alpha = jnp.dot(k, stacked, precision=HIGH, preferred_element_type=jnp.float32)
        o_ref[:, cols] = o_ref[:, cols] + b_ref[:, cols] + alpha


def final_call(mixed, same_beta, coupling, xs):
    return pl.pallas_call(
        final_kernel,
        out_shape=jax.ShapeDtypeStruct(same_beta.shape, jnp.float32),
        in_specs=[VMEM] * (3 + len(xs)),
        out_specs=VMEM,
        name="final",
    )(mixed, same_beta, coupling, *xs)


def per_device(
    coeff,
    beta_blocks,
    block_list,
    alpha_blocks,
    partner_mask,
    exc_source,
    exc_pair,
    exc_parity,
    occupation,
    coulomb,
):
    g = lax.axis_index("grp")
    c = lax.axis_index("c")
    alpha_rows, beta_width = coeff.shape
    n_exc, row_count = exc_source.shape
    n_pair = coulomb.shape[0]

    def shift(value, k):
        return lax.ppermute(
            value, "grp", [(i, (i - k) % N_GRP) for i in range(N_GRP)]
        )

    def swap(value):
        return lax.ppermute(value, "c", [(0, 1), (1, 0)])

    packed = pack(coeff)
    own = lax.all_to_all(packed, ("z", "x"), split_axis=0, concat_axis=0, tiled=True)
    own = own.reshape(NQ * 2 * RA, LANES)
    near = [own] + [shift(own, k) for k in range(1, N_GRP)]
    parts = near + [swap(v) for v in near]

    other_occ = swap(occupation)
    first = jnp.where(c == 0, occupation, other_occ)
    second = jnp.where(c == 0, other_occ, occupation)
    occ = jnp.concatenate([first, second], axis=1).astype(jnp.float32)
    weights = jnp.dot(coulomb, occ, precision=HIGH, preferred_element_type=jnp.float32)
    signed = jnp.concatenate([weights, -weights], axis=0)
    signed = jnp.pad(signed, ((0, 0), (0, 2 * LANES - COLS)))
    wtab = (
        signed.reshape(2 * n_pair // RA, RA, 2, LANES)
        .transpose(0, 2, 1, 3)
        .reshape(4 * n_pair, LANES)
    )

    rel_g = ((exc_source >> 9) - g) & (N_GRP - 1)
    rel_c = ((exc_source >> 3) & 1) ^ c
    pos = (rel_c * N_GRP + rel_g) * NQ + ((exc_source >> 4) & (NQ - 1))
    cidx = (pos * (2 * RA) + (exc_source & (RA - 1))).reshape(-1)
    pair = exc_pair + n_pair * exc_parity
    widx = ((pair >> 3) * (2 * RA) + (pair & (RA - 1))).reshape(-1)

    mixed_local = mixed_call(
        c.reshape(1).astype(jnp.int32), cidx, widx, wtab, parts, n_exc, row_count
    )
    mixed = lax.all_to_all(
        mixed_local.reshape(NQ, 2, RA, LANES),
        ("z", "x"),
        split_axis=0,
        concat_axis=0,
        tiled=True,
    )

    block_size = beta_blocks.shape[1]
    block_count = beta_width // block_size
    blocked = coeff.reshape(alpha_rows, block_count, block_size)
    block_ids = jnp.arange(block_count, dtype=jnp.int32)
    choosing = (block_list[0][:, None] == block_ids[None, :]).astype(jnp.float32)
    picked = jnp.einsum("rnk,pn->rpk", blocked, choosing, precision=HIGH)
    applied = jnp.einsum("rpk,pkl->rpl", picked, beta_blocks, precision=HIGH)
    placing = (block_list[1][:, None] == block_ids[None, :]).astype(jnp.float32)
    same_beta = jnp.einsum("rpl,pn->rnl", applied, placing, precision=HIGH).reshape(
        alpha_rows, beta_width
    )

    masked = alpha_blocks[0] * partner_mask[0][:, None, None].astype(jnp.float32)
    masked = jnp.roll(masked, -g, axis=0)
    coupling = masked.transpose(1, 0, 2).reshape(alpha_rows, N_GRP * alpha_rows)
    rows = [coeff] + [shift(coeff, k) for k in range(1, N_GRP)]
    return final_call(mixed, same_beta, coupling, rows)


def solution(mesh):
    fine = Mesh(mesh.devices.reshape(N_GRP, NZ, NX, NC), ("grp", "z", "x", "c"))
    wide = ("z", "x", "c")
    every = ("grp",) + wide
    in_specs = (
        P(every, None),
        P(),
        P(),
        P(every, None, None, None),
        P(every, None),
        P(None, "grp"),
        P(None, "grp"),
        P(None, "grp"),
        P(None, wide),
        P(),
    )
    return jax.shard_map(
        per_device,
        mesh=fine,
        in_specs=in_specs,
        out_specs=P(every, None),
        check_vma=False,
    )
```

```python
import functools

import jax
import jax.numpy as jnp
from jax import lax
from jax.experimental import pallas as pl
from jax.experimental.pallas import tpu as pltpu
from jax.sharding import Mesh
from jax.sharding import PartitionSpec as P

HIGH = lax.Precision.HIGHEST
RA = 8
LANES = 128
N_GRP = 4
NZ, NX, NC = 8, 4, 2
NQ = NZ * NX
COLS = 192
PAD = 8

SMEM = pl.BlockSpec(memory_space=pltpu.SMEM)
VMEM = pl.BlockSpec(memory_space=pltpu.VMEM)
ANY = pl.BlockSpec(memory_space=pl.ANY)


def pack_kernel(g_ref, mask_ref, x_ref, alpha_ref, o_ref):
    tail = COLS - LANES
    pieces = [jnp.zeros((RA, tail), jnp.float32)]
    for rel in range(N_GRP):
        h = (g_ref[0] + rel) & (N_GRP - 1)
        pieces.append(alpha_ref[0, h] * mask_ref[0, h].astype(jnp.float32))
    pieces.append(jnp.zeros((RA, LANES - tail - N_GRP * RA), jnp.float32))
    coupling = jnp.concatenate(pieces, axis=1)
    for j in range(NQ):
        lo = COLS * j
        o_ref[j, 0] = x_ref[:, lo : lo + LANES]
        o_ref[j, 1] = jnp.concatenate(
            [x_ref[:, lo + LANES : lo + COLS], coupling[:, tail:]], axis=1
        )


def pack(group, mask, coeff, alpha_blocks):
    return pl.pallas_call(
        pack_kernel,
        out_shape=jax.ShapeDtypeStruct((NQ, 2, RA, LANES), jnp.float32),
        in_specs=[SMEM, SMEM, VMEM, VMEM],
        out_specs=VMEM,
        name="pack",
    )(group, mask, coeff, alpha_blocks)


def mixed_kernel(n_exc, row_count, chunks, c_ref, cidx_hbm, widx_hbm, w_ref, *rest):
    parts = rest[: 2 * N_GRP]
    o_ref, table, cidx, widx, part_sem, idx_sem = rest[2 * N_GRP :]
    part_rows = NQ * 2 * RA
    per = n_exc // chunks
    length = per * row_count

    def index_copies(k):
        at = pl.ds(k * length, length)
        return (
            pltpu.make_async_copy(cidx_hbm.at[at], cidx.at[at], idx_sem.at[0, k]),
            pltpu.make_async_copy(widx_hbm.at[at], widx.at[at], idx_sem.at[1, k]),
        )

    for copy in index_copies(0):
        copy.start()
    copies = [
        pltpu.make_async_copy(
            part, table.at[pl.ds(i * part_rows, part_rows)], part_sem.at[i]
        )
        for i, part in enumerate(parts)
    ]
    for copy in copies:
        copy.start()
    for k in range(1, chunks):
        for copy in index_copies(k):
            copy.start()
    for copy in copies:
        copy.wait()
    core = c_ref[0]
    span = row_count - RA + 1

    def gather(q, offset, a, acc):
        start = q * (2 * RA) + core * RA + offset
        size = span + (n_exc - per) * row_count
        for e in range(per):
            base = e * row_count + a
            ci = cidx.at[pl.ds(base, size)][start]
            wi = widx.at[pl.ds(base, size)][start]
            term = (
                table[pl.ds(ci, 2, stride=RA), :] * w_ref[pl.ds(wi, 2, stride=RA), :]
            )
            acc = term if acc is None else acc + term
        return acc

    def first_block(q, carry):
        for a in range(RA):
            rows = pl.ds(q * (2 * RA) + a, 2, stride=RA)
            o_ref[rows, :] = gather(q, 0, a, None)
        at = q * (2 * RA)
        mix = table[pl.ds(pl.multiple_of(at + RA, RA), RA), :]
        mix = mix[:, COLS - LANES : COLS - LANES + N_GRP * RA]
        for half in range(2):
            rows = [
                table[pl.ds(pl.multiple_of(at + h * part_rows + half * RA, RA), RA), :]
                for h in range(N_GRP)
            ]
            alpha = jnp.dot(
                mix,
                jnp.concatenate(rows, axis=0),
                precision=HIGH,
                preferred_element_type=jnp.float32,
            )
            target = pl.ds(pl.multiple_of(at + half * RA, RA), RA)
            o_ref[target, :] = o_ref[target, :] + alpha
        return carry

    def later_chunk(k, carry):
        for copy in index_copies(k):
            copy.wait()

        def block(q, inner):
            for a in range(RA):
                rows = pl.ds(q * (2 * RA) + a, 2, stride=RA)
                o_ref[rows, :] = gather(q, k * length, a, o_ref[rows, :])
            return inner

        return lax.fori_loop(0, NQ, block, carry)

    for copy in index_copies(0):
        copy.wait()
    lax.fori_loop(0, NQ, first_block, 0)
    lax.fori_loop(1, chunks, later_chunk, 0)


def mixed_call(core, cidx, widx, wtab, parts, n_exc, row_count, chunks=3):
    part_rows = NQ * 2 * RA
    return pl.pallas_call(
        functools.partial(mixed_kernel, n_exc, row_count, chunks),
        out_shape=jax.ShapeDtypeStruct((part_rows, LANES), jnp.float32),
        in_specs=[SMEM, ANY, ANY, VMEM] + [ANY] * len(parts),
        out_specs=VMEM,
        scratch_shapes=[
            pltpu.VMEM((2 * N_GRP * part_rows, LANES), jnp.float32),
            pltpu.SMEM((n_exc * row_count,), jnp.int32),
            pltpu.SMEM((n_exc * row_count,), jnp.int32),
            pltpu.SemaphoreType.DMA((2 * N_GRP,)),
            pltpu.SemaphoreType.DMA((2, chunks)),
        ],
        compiler_params=pltpu.CompilerParams(vmem_limit_bytes=16 << 20),
        cost_estimate=pl.CostEstimate(
            flops=n_exc * row_count * COLS, bytes_accessed=8 << 20, transcendentals=0
        ),
        name="mixed",
    )(core, cidx, widx, wtab, *parts)


def final_kernel(m_ref, b_ref, o_ref):
    for j in range(NQ):
        lo = COLS * j
        o_ref[:, lo : lo + LANES] = m_ref[j, 0] + b_ref[:, lo : lo + LANES]
        o_ref[:, lo + LANES : lo + COLS] = (
            m_ref[j, 1, :, : COLS - LANES] + b_ref[:, lo + LANES : lo + COLS]
        )


def final_call(mixed, same_beta):
    return pl.pallas_call(
        final_kernel,
        out_shape=jax.ShapeDtypeStruct(same_beta.shape, jnp.float32),
        in_specs=[VMEM] * 2,
        out_specs=VMEM,
        name="final",
    )(mixed, same_beta)


def per_device(
    coeff,
    beta_blocks,
    block_list,
    alpha_blocks,
    partner_mask,
    exc_source,
    exc_pair,
    exc_parity,
    occupation,
    coulomb,
):
    g = lax.axis_index("grp")
    c = lax.axis_index("c")
    alpha_rows, beta_width = coeff.shape
    n_exc, row_count = exc_source.shape
    n_pair = coulomb.shape[0]

    def shift(value, k):
        return lax.ppermute(
            value, "grp", [(i, (i - k) % N_GRP) for i in range(N_GRP)]
        )

    def swap(value):
        return lax.ppermute(value, "c", [(0, 1), (1, 0)])

    packed = pack(g.reshape(1), partner_mask, coeff, alpha_blocks)
    own = lax.all_to_all(packed, ("z", "x"), split_axis=0, concat_axis=0, tiled=True)
    own = own.reshape(NQ * 2 * RA, LANES)

    other_occ = swap(occupation)
    first = jnp.where(c == 0, occupation, other_occ)
    second = jnp.where(c == 0, other_occ, occupation)
    occ = jnp.concatenate([first, second], axis=1).astype(jnp.float32)
    weights = jnp.dot(coulomb, occ, precision=HIGH, preferred_element_type=jnp.float32)
    signed = jnp.concatenate([weights, -weights], axis=0)
    signed = jnp.pad(signed, ((0, 0), (0, 2 * LANES - COLS)))
    wtab = (
        signed.reshape(2 * n_pair // RA, RA, 2, LANES)
        .transpose(0, 2, 1, 3)
        .reshape(4 * n_pair, LANES)
    )

    rel_g = ((exc_source >> 9) - g) & (N_GRP - 1)
    rel_c = ((exc_source >> 3) & 1) ^ c
    pos = (rel_c * N_GRP + rel_g) * NQ + ((exc_source >> 4) & (NQ - 1))
    cidx = (pos * (2 * RA) + (exc_source & (RA - 1))).reshape(-1)
    pair = exc_pair + n_pair * exc_parity
    widx = ((pair >> 3) * (2 * RA) + (pair & (RA - 1))).reshape(-1)

    own, wtab, cidx, widx, late = lax.optimization_barrier(
        (own, wtab, cidx, widx, coeff)
    )
    near = [own] + [shift(own, k) for k in range(1, N_GRP)]
    parts = near + [swap(v) for v in near]
    mixed_local = mixed_call(
        c.reshape(1).astype(jnp.int32), cidx, widx, wtab, parts, n_exc, row_count
    )
    mixed = lax.all_to_all(
        mixed_local.reshape(NQ, 2, RA, LANES),
        ("z", "x"),
        split_axis=0,
        concat_axis=0,
        tiled=True,
    )

    block_size = beta_blocks.shape[1]
    block_count = beta_width // block_size
    blocked = late.reshape(alpha_rows, block_count, block_size)
    block_ids = jnp.arange(block_count, dtype=jnp.int32)
    choosing = (block_list[0][:, None] == block_ids[None, :]).astype(jnp.float32)
    picked = jnp.einsum("rnk,pn->rpk", blocked, choosing, precision=HIGH)
    applied = jnp.einsum("rpk,pkl->rpl", picked, beta_blocks, precision=HIGH)
    placing = (block_list[1][:, None] == block_ids[None, :]).astype(jnp.float32)
    same_beta = jnp.einsum("rpl,pn->rnl", applied, placing, precision=HIGH).reshape(
        alpha_rows, beta_width
    )

    return final_call(mixed, same_beta)


def solution(mesh):
    fine = Mesh(mesh.devices.reshape(N_GRP, NZ, NX, NC), ("grp", "z", "x", "c"))
    wide = ("z", "x", "c")
    every = ("grp",) + wide
    in_specs = (
        P(every, None),
        P(),
        P(),
        P(every, None, None, None),
        P(every, None),
        P(None, "grp"),
        P(None, "grp"),
        P(None, "grp"),
        P(None, wide),
        P(),
    )
    return jax.shard_map(
        per_device,
        mesh=fine,
        in_specs=in_specs,
        out_specs=P(every, None),
        check_vma=False,
    )
```

```python
import functools

import jax
import jax.numpy as jnp
from jax import lax
from jax.experimental import pallas as pl
from jax.experimental.pallas import tpu as pltpu
from jax.sharding import Mesh
from jax.sharding import PartitionSpec as P

HIGH = lax.Precision.HIGHEST
RA = 8
LANES = 128
N_GRP = 4
NZ, NXH, NXL, NC = 8, 2, 2, 2
NQ = NZ * NXH
NS = NXL * NC
NT = 3
PART = NQ * NT * RA

SMEM = pl.BlockSpec(memory_space=pltpu.SMEM)
VMEM = pl.BlockSpec(memory_space=pltpu.VMEM)
ANY = pl.BlockSpec(memory_space=pl.ANY)


def pack_kernel(g_ref, mask_ref, x_ref, alpha_ref, o_ref):
    pieces = []
    for rel in range(N_GRP):
        h = (g_ref[0] + rel) & (N_GRP - 1)
        pieces.append(alpha_ref[0, h] * mask_ref[0, h].astype(jnp.float32))
    pieces.append(jnp.zeros((RA, LANES - N_GRP * RA), jnp.float32))
    coupling = jnp.concatenate(pieces, axis=1)
    for j in range(NQ):
        for t in range(NT):
            lo = (j * NT + t) * LANES
            o_ref[j, t] = x_ref[:, lo : lo + LANES]
        o_ref[j, NT] = coupling


def pack(group, mask, coeff, alpha_blocks):
    return pl.pallas_call(
        pack_kernel,
        out_shape=jax.ShapeDtypeStruct((NQ, NT + 1, RA, LANES), jnp.float32),
        in_specs=[SMEM, SMEM, VMEM, VMEM],
        out_specs=VMEM,
        name="pack",
    )(group, mask, coeff, alpha_blocks)


def mixed_kernel(
    n_exc, row_count, chunks, sel_ref, cidx_hbm, widx_hbm, w_ref, mix_ref, *rest
):
    count = N_GRP * NS
    parts = rest[:count]
    o_ref, table, cidx, widx, part_sem, idx_sem = rest[count:]
    per = n_exc // chunks
    length = per * row_count

    def index_copies(k):
        at = pl.ds(k * length, length)
        return (
            pltpu.make_async_copy(cidx_hbm.at[at], cidx.at[at], idx_sem.at[0, k]),
            pltpu.make_async_copy(widx_hbm.at[at], widx.at[at], idx_sem.at[1, k]),
        )

    for copy in index_copies(0):
        copy.start()
    copies = [
        pltpu.make_async_copy(part, table.at[pl.ds(i * PART, PART)], part_sem.at[i])
        for i, part in enumerate(parts)
    ]
    for copy in copies:
        copy.start()
    for k in range(1, chunks):
        for copy in index_copies(k):
            copy.start()
    for copy in copies:
        copy.wait()
    shift = sel_ref[0] * RA
    size = row_count - RA + 1 + (n_exc - per) * row_count

    def gather(q, offset, a, acc):
        start = q * (NS * RA) + shift + offset
        for e in range(per):
            base = e * row_count + a
            ci = cidx.at[pl.ds(base, size)][start]
            wi = widx.at[pl.ds(base, size)][start]
            term = (
                table[pl.ds(ci, NT, stride=RA), :] * w_ref[pl.ds(wi, NT, stride=RA), :]
            )
            acc = term if acc is None else acc + term
        return acc

    def first_block(q, carry):
        for a in range(RA):
            rows = pl.ds(q * (NT * RA) + a, NT, stride=RA)
            o_ref[rows, :] = gather(q, 0, a, None)
        mix = mix_ref[q, NT][:, : N_GRP * RA]
        for t in range(NT):
            at = q * (NT * RA) + t * RA
            rows = [
                table[pl.ds(pl.multiple_of(at + h * PART, RA), RA), :]
                for h in range(N_GRP)
            ]
            alpha = jnp.dot(
                mix,
                jnp.concatenate(rows, axis=0),
                precision=HIGH,
                preferred_element_type=jnp.float32,
            )
            target = pl.ds(pl.multiple_of(at, RA), RA)
            o_ref[target, :] = o_ref[target, :] + alpha
        return carry

    def later_chunk(k, carry):
        for copy in index_copies(k):
            copy.wait()

        def block(q, inner):
            for a in range(RA):
                rows = pl.ds(q * (NT * RA) + a, NT, stride=RA)
                o_ref[rows, :] = gather(q, k * length, a, o_ref[rows, :])
            return inner

        return lax.fori_loop(0, NQ, block, carry)

    for copy in index_copies(0):
        copy.wait()
    lax.fori_loop(0, NQ, first_block, 0)
    lax.fori_loop(1, chunks, later_chunk, 0)


def mixed_call(sel, cidx, widx, wtab, mix, parts, n_exc, row_count, chunks=3):
    count = N_GRP * NS
    return pl.pallas_call(
        functools.partial(mixed_kernel, n_exc, row_count, chunks),
        out_shape=jax.ShapeDtypeStruct((PART, LANES), jnp.float32),
        in_specs=[SMEM, ANY, ANY, VMEM, VMEM] + [ANY] * count,
        out_specs=VMEM,
        scratch_shapes=[
            pltpu.VMEM((count * PART, LANES), jnp.float32),
            pltpu.SMEM((n_exc * row_count,), jnp.int32),
            pltpu.SMEM((n_exc * row_count,), jnp.int32),
            pltpu.SemaphoreType.DMA((count,)),
            pltpu.SemaphoreType.DMA((2, chunks)),
        ],
        compiler_params=pltpu.CompilerParams(vmem_limit_bytes=16 << 20),
        cost_estimate=pl.CostEstimate(
            flops=n_exc * row_count * NT * LANES // 2,
            bytes_accessed=8 << 20,
            transcendentals=0,
        ),
        name="mixed",
    )(sel, cidx, widx, wtab, mix, *parts)


def per_device(
    coeff,
    beta_blocks,
    block_list,
    alpha_blocks,
    partner_mask,
    exc_source,
    exc_pair,
    exc_parity,
    occupation,
    coulomb,
):
    g = lax.axis_index("grp")
    xl = lax.axis_index("xl")
    c = lax.axis_index("c")
    alpha_rows, beta_width = coeff.shape
    n_exc, row_count = exc_source.shape
    n_pair = coulomb.shape[0]

    def shift(value, k):
        return lax.ppermute(
            value, "grp", [(i, (i - k) % N_GRP) for i in range(N_GRP)]
        )

    def swap(value, axis):
        return lax.ppermute(value, axis, [(0, 1), (1, 0)])

    packed = pack(g.reshape(1), partner_mask, coeff, alpha_blocks)
    arrived = lax.all_to_all(
        packed, ("z", "xh"), split_axis=0, concat_axis=0, tiled=True
    )

    sel = xl * NC + c
    pieces = [
        lax.ppermute(occupation, ("xl", "c"), [(i, i ^ k) for i in range(NS)])
        for k in range(1, NS)
    ]
    pieces = jnp.stack([occupation] + pieces)
    ordered = [
        lax.dynamic_index_in_dim(pieces, sel ^ k, 0, keepdims=False) for k in range(NS)
    ]
    occ = jnp.concatenate(ordered, axis=1).astype(jnp.float32)
    weights = jnp.dot(coulomb, occ, precision=HIGH, preferred_element_type=jnp.float32)
    signed = jnp.concatenate([weights, -weights], axis=0)
    wtab = (
        signed.reshape(2 * n_pair // RA, RA, NT, LANES)
        .transpose(0, 2, 1, 3)
        .reshape(2 * n_pair * NT, LANES)
    )

    rel_g = ((exc_source >> 9) - g) & (N_GRP - 1)
    rel_s = ((exc_source >> 3) & (NS - 1)) ^ sel
    pos = (rel_s * N_GRP + rel_g) * NQ + ((exc_source >> 5) & (NQ - 1))
    cidx = (pos * (NT * RA) + (exc_source & (RA - 1))).reshape(-1)
    pair = exc_pair + n_pair * exc_parity
    widx = ((pair >> 3) * (NT * RA) + (pair & (RA - 1))).reshape(-1)

    arrived, wtab, cidx, widx, late = lax.optimization_barrier(
        (arrived, wtab, cidx, widx, coeff)
    )
    own = arrived[:, :NT].reshape(PART, LANES)
    near = [own] + [shift(own, k) for k in range(1, N_GRP)]
    across = [swap(near[0], "xl"), swap(near[1], "xl"), None, swap(near[3], "xl")]
    across[2] = shift(across[0], 2)
    parts = (
        near
        + [swap(v, "c") for v in near]
        + across
        + [swap(v, "c") for v in across]
    )
    mixed_local = mixed_call(
        sel.reshape(1).astype(jnp.int32),
        cidx,
        widx,
        wtab,
        arrived,
        parts,
        n_exc,
        row_count,
    )
    mixed = lax.all_to_all(
        mixed_local.reshape(NQ, NT, RA, LANES),
        ("z", "xh"),
        split_axis=0,
        concat_axis=0,
        tiled=True,
    )
    mixed = (
        mixed.reshape(NQ * NT, RA, LANES).transpose(1, 0, 2).reshape(alpha_rows, -1)
    )

    block_size = beta_blocks.shape[1]
    block_count = beta_width // block_size
    blocked = late.reshape(alpha_rows, block_count, block_size)
    block_ids = jnp.arange(block_count, dtype=jnp.int32)
    choosing = (block_list[0][:, None] == block_ids[None, :]).astype(jnp.float32)
    picked = jnp.einsum("rnk,pn->rpk", blocked, choosing, precision=HIGH)
    applied = jnp.einsum("rpk,pkl->rpl", picked, beta_blocks, precision=HIGH)
    placing = (block_list[1][:, None] == block_ids[None, :]).astype(jnp.float32)
    same_beta = jnp.einsum("rpl,pn->rnl", applied, placing, precision=HIGH).reshape(
        alpha_rows, beta_width
    )

    return mixed + same_beta


def solution(mesh):
    wide = ("z", "xh", "xl", "c")
    fine = Mesh(mesh.devices.reshape(N_GRP, NZ, NXH, NXL, NC), ("grp",) + wide)
    every = ("grp",) + wide
    in_specs = (
        P(every, None),
        P(),
        P(),
        P(every, None, None, None),
        P(every, None),
        P(None, "grp"),
        P(None, "grp"),
        P(None, "grp"),
        P(None, wide),
        P(),
    )
    return jax.shard_map(
        per_device,
        mesh=fine,
        in_specs=in_specs,
        out_specs=P(every, None),
        check_vma=False,
    )
```

```python
import functools

import jax
import jax.numpy as jnp
from jax import lax
from jax.experimental import pallas as pl
from jax.experimental.pallas import tpu as pltpu
from jax.sharding import Mesh
from jax.sharding import PartitionSpec as P

HIGH = lax.Precision.HIGHEST
RA = 8
LANES = 128
N_GRP = 4
NZ, NXH, NXL, NC = 8, 2, 2, 2
NQ = NZ * NXH
NS = NXL * NC
NT = 3
PART = NQ * NT * RA
EPAD = 96
CHUNK = 32

SMEM = pl.BlockSpec(memory_space=pltpu.SMEM)
VMEM = pl.BlockSpec(memory_space=pltpu.VMEM)
ANY = pl.BlockSpec(memory_space=pl.ANY)


def pack_kernel(g_ref, mask_ref, x_ref, alpha_ref, o_ref):
    pieces = []
    for rel in range(N_GRP):
        h = (g_ref[0] + rel) & (N_GRP - 1)
        pieces.append(alpha_ref[0, h] * mask_ref[0, h].astype(jnp.float32))
    pieces.append(jnp.zeros((RA, LANES - N_GRP * RA), jnp.float32))
    coupling = jnp.concatenate(pieces, axis=1)
    for j in range(NQ):
        for t in range(NT):
            lo = (j * NT + t) * LANES
            o_ref[j, t] = x_ref[:, lo : lo + LANES]
        o_ref[j, NT] = coupling


def pack(group, mask, coeff, alpha_blocks):
    return pl.pallas_call(
        pack_kernel,
        out_shape=jax.ShapeDtypeStruct((NQ, NT + 1, RA, LANES), jnp.float32),
        in_specs=[SMEM, SMEM, VMEM, VMEM],
        out_specs=VMEM,
        name="pack",
    )(group, mask, coeff, alpha_blocks)


def prep_kernel(n_pair, place_ref, src_ref, pair_ref, par_ref, ci_ref, wi_ref):
    g, sel = place_ref[0], place_ref[1]
    n_exc, row_count = src_ref.shape
    row = lax.broadcasted_iota(jnp.int32, (LANES, row_count), 0)
    col = lax.broadcasted_iota(jnp.int32, (LANES, row_count), 1)
    want = (row >> 3) * (NS * RA) + sel * RA + (row & (RA - 1))
    pick = jnp.where(col == want, 1.0, 0.0)
    src = src_ref[...]
    rel_g = ((src >> 9) - g) & (N_GRP - 1)
    rel_s = ((src >> 3) & (NS - 1)) ^ sel
    pos = (rel_s * N_GRP + rel_g) * NQ + ((src >> 5) & (NQ - 1))
    pair = pair_ref[...] + n_pair * par_ref[...]
    for value, out in (
        (pos * (NT * RA) + (src & (RA - 1)), ci_ref),
        ((pair >> 3) * (NT * RA) + (pair & (RA - 1)), wi_ref),
    ):
        chosen = lax.dot_general(
            value.astype(jnp.float32),
            pick,
            (((1,), (1,)), ((), ())),
            precision=HIGH,
            preferred_element_type=jnp.float32,
        )
        out[pl.ds(0, n_exc), :] = (chosen + 0.5).astype(jnp.int32)
        out[pl.ds(n_exc, EPAD - n_exc), :] = jnp.zeros((EPAD - n_exc, LANES), jnp.int32)


def prep_call(place, src, pair, par, n_pair):
    shape = jax.ShapeDtypeStruct((EPAD, LANES), jnp.int32)
    ci, wi = pl.pallas_call(
        functools.partial(prep_kernel, n_pair),
        out_shape=(shape, shape),
        in_specs=[SMEM, VMEM, VMEM, VMEM],
        out_specs=(VMEM, VMEM),
        name="prep",
    )(place, src, pair, par)
    return ci.reshape(-1), wi.reshape(-1)


def mixed_kernel(n_exc, cidx_hbm, widx_hbm, w_ref, mix_ref, *rest):
    count = N_GRP * NS
    parts = rest[:count]
    o_ref, table, cidx, widx, idx_sem = rest[count:]
    chunks = EPAD // CHUNK
    length = CHUNK * LANES

    def index_copies(k):
        at = pl.ds(k * length, length)
        return (
            pltpu.make_async_copy(cidx_hbm.at[at], cidx.at[at], idx_sem.at[0, k]),
            pltpu.make_async_copy(widx_hbm.at[at], widx.at[at], idx_sem.at[1, k]),
        )

    for k in range(chunks):
        for copy in index_copies(k):
            copy.start()
    for i, part in enumerate(parts):
        table[pl.ds(i * PART, PART), :] = part[...]
    size = (NQ - 1) * RA + 1

    for k in range(chunks):
        for copy in index_copies(k):
            copy.wait()

        def block(q, carry, k=k):
            start = q * RA
            for a in range(RA):
                rows = pl.ds(q * (NT * RA) + a, NT, stride=RA)
                acc = None if k == 0 else o_ref[rows, :]
                for e in range(k * CHUNK, min((k + 1) * CHUNK, n_exc)):
                    base = e * LANES + a
                    ci = cidx.at[pl.ds(base, size)][start]
                    wi = widx.at[pl.ds(base, size)][start]
                    term = (
                        table[pl.ds(ci, NT, stride=RA), :]
                        * w_ref[pl.ds(wi, NT, stride=RA), :]
                    )
                    acc = term if acc is None else acc + term
                o_ref[rows, :] = acc
            if k == 0:
                mix = mix_ref[q, NT][:, : N_GRP * RA]
                for t in range(NT):
                    at = q * (NT * RA) + t * RA
                    stacked = [
                        table[pl.ds(pl.multiple_of(at + h * PART, RA), RA), :]
                        for h in range(N_GRP)
                    ]
                    alpha = jnp.dot(
                        mix,
                        jnp.concatenate(stacked, axis=0),
                        precision=HIGH,
                        preferred_element_type=jnp.float32,
                    )
                    target = pl.ds(pl.multiple_of(at, RA), RA)
                    o_ref[target, :] = o_ref[target, :] + alpha
            return carry

        lax.fori_loop(0, NQ, block, 0)


def mixed_call(cidx, widx, wtab, mix, parts, n_exc):
    count = N_GRP * NS
    index = pltpu.SMEM((EPAD * LANES,), jnp.int32)
    return pl.pallas_call(
        functools.partial(mixed_kernel, n_exc),
        out_shape=jax.ShapeDtypeStruct((PART, LANES), jnp.float32),
        in_specs=[ANY, ANY, VMEM, VMEM] + [VMEM] * count,
        out_specs=VMEM,
        scratch_shapes=[
            pltpu.VMEM((count * PART, LANES), jnp.float32),
            index,
            index,
            pltpu.SemaphoreType.DMA((2, EPAD // CHUNK)),
        ],
        compiler_params=pltpu.CompilerParams(vmem_limit_bytes=16 << 20),
        cost_estimate=pl.CostEstimate(
            flops=n_exc * NQ * RA * NT * LANES * 2,
            bytes_accessed=8 << 20,
            transcendentals=0,
        ),
        name="mixed",
    )(cidx, widx, wtab, mix, *parts)


def per_device(
    coeff,
    beta_blocks,
    block_list,
    alpha_blocks,
    partner_mask,
    exc_source,
    exc_pair,
    exc_parity,
    occupation,
    coulomb,
):
    g = lax.axis_index("grp")
    xl = lax.axis_index("xl")
    c = lax.axis_index("c")
    alpha_rows, beta_width = coeff.shape
    n_exc = exc_source.shape[0]
    n_pair = coulomb.shape[0]

    def shift(value, k):
        return lax.ppermute(
            value, "grp", [(i, (i - k) % N_GRP) for i in range(N_GRP)]
        )

    def swap(value, axis):
        return lax.ppermute(value, axis, [(0, 1), (1, 0)])

    packed = pack(g.reshape(1), partner_mask, coeff, alpha_blocks)
    arrived = lax.all_to_all(
        packed, ("z", "xh"), split_axis=0, concat_axis=0, tiled=True
    )

    sel = xl * NC + c
    pieces = [
        lax.ppermute(occupation, ("xl", "c"), [(i, i ^ k) for i in range(NS)])
        for k in range(1, NS)
    ]
    pieces = jnp.stack([occupation] + pieces)
    ordered = [
        lax.dynamic_index_in_dim(pieces, sel ^ k, 0, keepdims=False) for k in range(NS)
    ]
    occ = jnp.concatenate(ordered, axis=1).astype(jnp.float32)
    weights = jnp.dot(coulomb, occ, precision=HIGH, preferred_element_type=jnp.float32)
    signed = jnp.concatenate([weights, -weights], axis=0)
    wtab = (
        signed.reshape(2 * n_pair // RA, RA, NT, LANES)
        .transpose(0, 2, 1, 3)
        .reshape(2 * n_pair * NT, LANES)
    )

    place = jnp.stack([g, sel]).astype(jnp.int32)
    cidx, widx = prep_call(place, exc_source, exc_pair, exc_parity, n_pair)

    arrived, wtab, cidx, widx, late = lax.optimization_barrier(
        (arrived, wtab, cidx, widx, coeff)
    )
    own = arrived[:, :NT].reshape(PART, LANES)
    after, before = shift(own, 1), shift(own, N_GRP - 1)
    over = swap(own, "xl")
    again, over_again, after, before = lax.optimization_barrier(
        (own, over, after, before)
    )
    near = [own, after, shift(again, 2), before]
    across = [over, swap(after, "xl"), shift(over_again, 2), swap(before, "xl")]
    parts = (
        near
        + [swap(v, "c") for v in near]
        + across
        + [swap(v, "c") for v in across]
    )
    mixed_local = mixed_call(
        cidx,
        widx,
        wtab,
        arrived,
        parts,
        n_exc,
    )
    mixed = lax.all_to_all(
        mixed_local.reshape(NQ, NT, RA, LANES),
        ("z", "xh"),
        split_axis=0,
        concat_axis=0,
        tiled=True,
    )
    mixed = (
        mixed.reshape(NQ * NT, RA, LANES).transpose(1, 0, 2).reshape(alpha_rows, -1)
    )

    block_size = beta_blocks.shape[1]
    block_count = beta_width // block_size
    blocked = late.reshape(alpha_rows, block_count, block_size)
    block_ids = jnp.arange(block_count, dtype=jnp.int32)
    choosing = (block_list[0][:, None] == block_ids[None, :]).astype(jnp.float32)
    picked = jnp.einsum("rnk,pn->rpk", blocked, choosing, precision=HIGH)
    applied = jnp.einsum("rpk,pkl->rpl", picked, beta_blocks, precision=HIGH)
    placing = (block_list[1][:, None] == block_ids[None, :]).astype(jnp.float32)
    same_beta = jnp.einsum("rpl,pn->rnl", applied, placing, precision=HIGH).reshape(
        alpha_rows, beta_width
    )

    return mixed + same_beta


def solution(mesh):
    wide = ("z", "xh", "xl", "c")
    fine = Mesh(mesh.devices.reshape(N_GRP, NZ, NXH, NXL, NC), ("grp",) + wide)
    every = ("grp",) + wide
    in_specs = (
        P(every, None),
        P(),
        P(),
        P(every, None, None, None),
        P(every, None),
        P(None, "grp"),
        P(None, "grp"),
        P(None, "grp"),
        P(None, wide),
        P(),
    )
    return jax.shard_map(
        per_device,
        mesh=fine,
        in_specs=in_specs,
        out_specs=P(every, None),
        check_vma=False,
    )
```

```python
import functools

import jax
import jax.numpy as jnp
from jax import lax
from jax.experimental import pallas as pl
from jax.experimental.pallas import tpu as pltpu
from jax.sharding import Mesh
from jax.sharding import PartitionSpec as P

HIGH = lax.Precision.HIGHEST
RA = 8
LANES = 128
N_GRP = 4
NZ, NXH, NXL, NC = 8, 2, 2, 2
NQ = NZ * NXH
NS = NXL * NC
NT = 3
PART = NQ * NT * RA
EPAD = 96
CHUNK = 32

SMEM = pl.BlockSpec(memory_space=pltpu.SMEM)
VMEM = pl.BlockSpec(memory_space=pltpu.VMEM)
HBM = pl.BlockSpec(memory_space=pltpu.HBM)


def pack_kernel(g_ref, mask_ref, x_ref, alpha_ref, o_ref):
    pieces = []
    for rel in range(N_GRP):
        h = (g_ref[0] + rel) & (N_GRP - 1)
        pieces.append(alpha_ref[0, h] * mask_ref[0, h].astype(jnp.float32))
    pieces.append(jnp.zeros((RA, LANES - N_GRP * RA), jnp.float32))
    coupling = jnp.concatenate(pieces, axis=1)
    for j in range(NQ):
        for t in range(NT):
            lo = (j * NT + t) * LANES
            o_ref[j, t] = x_ref[:, lo : lo + LANES]
        o_ref[j, NT] = coupling


def pack(group, mask, coeff, alpha_blocks):
    return pl.pallas_call(
        pack_kernel,
        out_shape=jax.ShapeDtypeStruct((NQ, NT + 1, RA, LANES), jnp.float32),
        in_specs=[SMEM, SMEM, VMEM, VMEM],
        out_specs=VMEM,
        name="pack",
    )(group, mask, coeff, alpha_blocks)


def prep_kernel(n_pair, place_ref, src_ref, pair_ref, par_ref, ci_ref, wi_ref):
    g, sel = place_ref[0], place_ref[1]
    n_exc, row_count = src_ref.shape
    row = lax.broadcasted_iota(jnp.int32, (LANES, row_count), 0)
    col = lax.broadcasted_iota(jnp.int32, (LANES, row_count), 1)
    want = (row >> 3) * (NS * RA) + sel * RA + (row & (RA - 1))
    pick = jnp.where(col == want, 1.0, 0.0)
    src = src_ref[...]
    rel_g = ((src >> 9) - g) & (N_GRP - 1)
    rel_s = ((src >> 3) & (NS - 1)) ^ sel
    pos = (rel_s * N_GRP + rel_g) * NQ + ((src >> 5) & (NQ - 1))
    pair = pair_ref[...] + n_pair * par_ref[...]
    for value, out in (
        (pos * (NT * RA) + (src & (RA - 1)), ci_ref),
        ((pair >> 3) * (NT * RA) + (pair & (RA - 1)), wi_ref),
    ):
        chosen = lax.dot_general(
            value.astype(jnp.float32),
            pick,
            (((1,), (1,)), ((), ())),
            precision=HIGH,
            preferred_element_type=jnp.float32,
        )
        out[pl.ds(0, n_exc), :] = (chosen + 0.5).astype(jnp.int32)
        out[pl.ds(n_exc, EPAD - n_exc), :] = jnp.zeros((EPAD - n_exc, LANES), jnp.int32)


def prep_call(place, src, pair, par, n_pair):
    shape = jax.ShapeDtypeStruct((EPAD, LANES), jnp.int32)
    ci, wi = pl.pallas_call(
        functools.partial(prep_kernel, n_pair),
        out_shape=(shape, shape),
        in_specs=[SMEM, VMEM, VMEM, VMEM],
        out_specs=(VMEM, VMEM),
        name="prep",
    )(place, src, pair, par)
    return tuple(
        pltpu.with_memory_space_constraint(v.reshape(-1), pltpu.HBM) for v in (ci, wi)
    )


def mixed_kernel(n_exc, cidx_hbm, widx_hbm, w_ref, mix_ref, *rest):
    count = N_GRP * NS
    parts = rest[:count]
    o_ref, table, cidx, widx, idx_sem = rest[count:]
    chunks = EPAD // CHUNK
    length = CHUNK * LANES

    def index_copies(k):
        at = pl.ds(k * length, length)
        return (
            pltpu.make_async_copy(cidx_hbm.at[at], cidx.at[at], idx_sem.at[0, k]),
            pltpu.make_async_copy(widx_hbm.at[at], widx.at[at], idx_sem.at[1, k]),
        )

    for k in range(chunks):
        for copy in index_copies(k):
            copy.start()
    for i, part in enumerate(parts):
        table[pl.ds(i * PART, PART), :] = part[...]
    size = (NQ - 1) * RA + 1

    for k in range(chunks):
        for copy in index_copies(k):
            copy.wait()

        def block(q, carry, k=k):
            start = q * RA
            for a in range(RA):
                rows = pl.ds(q * (NT * RA) + a, NT, stride=RA)
                acc = None if k == 0 else o_ref[rows, :]
                for e in range(k * CHUNK, min((k + 1) * CHUNK, n_exc)):
                    base = e * LANES + a
                    ci = cidx.at[pl.ds(base, size)][start]
                    wi = widx.at[pl.ds(base, size)][start]
                    term = (
                        table[pl.ds(ci, NT, stride=RA), :]
                        * w_ref[pl.ds(wi, NT, stride=RA), :]
                    )
                    acc = term if acc is None else acc + term
                o_ref[rows, :] = acc
            if k == 0:
                mix = mix_ref[q, NT][:, : N_GRP * RA]
                for t in range(NT):
                    at = q * (NT * RA) + t * RA
                    stacked = [
                        table[pl.ds(pl.multiple_of(at + h * PART, RA), RA), :]
                        for h in range(N_GRP)
                    ]
                    alpha = jnp.dot(
                        mix,
                        jnp.concatenate(stacked, axis=0),
                        precision=HIGH,
                        preferred_element_type=jnp.float32,
                    )
                    target = pl.ds(pl.multiple_of(at, RA), RA)
                    o_ref[target, :] = o_ref[target, :] + alpha
            return carry

        lax.fori_loop(0, NQ, block, 0)


def mixed_call(cidx, widx, wtab, mix, parts, n_exc):
    count = N_GRP * NS
    index = pltpu.SMEM((EPAD * LANES,), jnp.int32)
    return pl.pallas_call(
        functools.partial(mixed_kernel, n_exc),
        out_shape=jax.ShapeDtypeStruct((PART, LANES), jnp.float32),
        in_specs=[HBM, HBM, VMEM, VMEM] + [VMEM] * count,
        out_specs=VMEM,
        scratch_shapes=[
            pltpu.VMEM((count * PART, LANES), jnp.float32),
            index,
            index,
            pltpu.SemaphoreType.DMA((2, EPAD // CHUNK)),
        ],
        compiler_params=pltpu.CompilerParams(vmem_limit_bytes=16 << 20),
        cost_estimate=pl.CostEstimate(
            flops=n_exc * NQ * RA * NT * LANES * 2,
            bytes_accessed=8 << 20,
            transcendentals=0,
        ),
        name="mixed",
    )(cidx, widx, wtab, mix, *parts)


def per_device(
    coeff,
    beta_blocks,
    block_list,
    alpha_blocks,
    partner_mask,
    exc_source,
    exc_pair,
    exc_parity,
    occupation,
    coulomb,
):
    g = lax.axis_index("grp")
    xl = lax.axis_index("xl")
    c = lax.axis_index("c")
    alpha_rows, beta_width = coeff.shape
    n_exc = exc_source.shape[0]
    n_pair = coulomb.shape[0]

    def shift(value, k):
        return lax.ppermute(
            value, "grp", [(i, (i - k) % N_GRP) for i in range(N_GRP)]
        )

    def swap(value, axis):
        return lax.ppermute(value, axis, [(0, 1), (1, 0)])

    packed = pack(g.reshape(1), partner_mask, coeff, alpha_blocks)
    arrived = lax.all_to_all(
        packed, ("z", "xh"), split_axis=0, concat_axis=0, tiled=True
    )

    sel = xl * NC + c
    place = jnp.stack([g, sel]).astype(jnp.int32)
    cidx, widx = prep_call(place, exc_source, exc_pair, exc_parity, n_pair)
    pieces = [
        lax.ppermute(occupation, ("xl", "c"), [(i, i ^ k) for i in range(NS)])
        for k in range(1, NS)
    ]
    pieces = jnp.stack([occupation] + pieces)
    ordered = [
        lax.dynamic_index_in_dim(pieces, sel ^ k, 0, keepdims=False) for k in range(NS)
    ]
    occ = jnp.concatenate(ordered, axis=1).astype(jnp.float32)
    weights = jnp.dot(coulomb, occ, precision=HIGH, preferred_element_type=jnp.float32)
    signed = jnp.concatenate([weights, -weights], axis=0)
    wtab = (
        signed.reshape(2 * n_pair // RA, RA, NT, LANES)
        .transpose(0, 2, 1, 3)
        .reshape(2 * n_pair * NT, LANES)
    )

    block_size = beta_blocks.shape[1]
    block_count = beta_width // block_size
    blocked = coeff.reshape(alpha_rows, block_count, block_size)
    block_ids = jnp.arange(block_count, dtype=jnp.int32)
    choosing = (block_list[0][:, None] == block_ids[None, :]).astype(jnp.float32)
    picked = jnp.einsum("rnk,pn->rpk", blocked, choosing, precision=HIGH)
    arrived, wtab, cidx, widx, picked = lax.optimization_barrier(
        (arrived, wtab, cidx, widx, picked)
    )
    own = arrived[:, :NT].reshape(PART, LANES)
    after, before = shift(own, 1), shift(own, N_GRP - 1)
    over = swap(own, "xl")
    again, over_again, after, before = lax.optimization_barrier(
        (own, over, after, before)
    )
    near = [own, after, shift(again, 2), before]
    across = [over, swap(after, "xl"), shift(over_again, 2), swap(before, "xl")]
    parts = (
        near
        + [swap(v, "c") for v in near]
        + across
        + [swap(v, "c") for v in across]
    )
    mixed_local = mixed_call(
        cidx,
        widx,
        wtab,
        arrived,
        parts,
        n_exc,
    )
    mixed = lax.all_to_all(
        mixed_local.reshape(NQ, NT, RA, LANES),
        ("z", "xh"),
        split_axis=0,
        concat_axis=0,
        tiled=True,
    )
    mixed = (
        mixed.reshape(NQ * NT, RA, LANES).transpose(1, 0, 2).reshape(alpha_rows, -1)
    )

    applied = jnp.einsum("rpk,pkl->rpl", picked, beta_blocks, precision=HIGH)
    placing = (block_list[1][:, None] == block_ids[None, :]).astype(jnp.float32)
    same_beta = jnp.einsum("rpl,pn->rnl", applied, placing, precision=HIGH).reshape(
        alpha_rows, beta_width
    )

    return mixed + same_beta


def solution(mesh):
    wide = ("z", "xh", "xl", "c")
    fine = Mesh(mesh.devices.reshape(N_GRP, NZ, NXH, NXL, NC), ("grp",) + wide)
    every = ("grp",) + wide
    in_specs = (
        P(every, None),
        P(),
        P(),
        P(every, None, None, None),
        P(every, None),
        P(None, "grp"),
        P(None, "grp"),
        P(None, "grp"),
        P(None, wide),
        P(),
    )
    return jax.shard_map(
        per_device,
        mesh=fine,
        in_specs=in_specs,
        out_specs=P(every, None),
        check_vma=False,
    )
```

```python
import functools

import jax
import jax.numpy as jnp
from jax import lax
from jax.experimental import pallas as pl
from jax.experimental.pallas import tpu as pltpu
from jax.sharding import Mesh
from jax.sharding import PartitionSpec as P

HIGH = lax.Precision.HIGHEST
RA = 8
LANES = 128
N_GRP = 4
NZ, NXH, NXL, NC = 8, 2, 2, 2
NQ = NZ * NXH
NS = NXL * NC
NT = 3
PART = NQ * NT * RA
EPAD = 96
CHUNK = 32

SMEM = pl.BlockSpec(memory_space=pltpu.SMEM)
VMEM = pl.BlockSpec(memory_space=pltpu.VMEM)
HBM = pl.BlockSpec(memory_space=pltpu.HBM)


def pack_kernel(g_ref, mask_ref, x_ref, alpha_ref, o_ref):
    pieces = []
    for rel in range(N_GRP):
        h = (g_ref[0] + rel) & (N_GRP - 1)
        pieces.append(alpha_ref[0, h] * mask_ref[0, h].astype(jnp.float32))
    pieces.append(jnp.zeros((RA, LANES - N_GRP * RA), jnp.float32))
    coupling = jnp.concatenate(pieces, axis=1)
    for j in range(NQ):
        for t in range(NT):
            lo = (j * NT + t) * LANES
            o_ref[j, t] = x_ref[:, lo : lo + LANES]
        o_ref[j, NT] = coupling


def pack(group, mask, coeff, alpha_blocks):
    return pl.pallas_call(
        pack_kernel,
        out_shape=jax.ShapeDtypeStruct((NQ, NT + 1, RA, LANES), jnp.float32),
        in_specs=[SMEM, SMEM, VMEM, VMEM],
        out_specs=VMEM,
        name="pack",
    )(group, mask, coeff, alpha_blocks)


def prep_kernel(n_pair, place_ref, src_ref, pair_ref, par_ref, ci_ref, wi_ref):
    g, sel = place_ref[0], place_ref[1]
    n_exc, row_count = src_ref.shape
    row = lax.broadcasted_iota(jnp.int32, (LANES, row_count), 0)
    col = lax.broadcasted_iota(jnp.int32, (LANES, row_count), 1)
    want = (row >> 3) * (NS * RA) + sel * RA + (row & (RA - 1))
    pick = jnp.where(col == want, 1.0, 0.0)
    src = src_ref[...]
    rel_g = ((src >> 9) - g) & (N_GRP - 1)
    rel_s = ((src >> 3) & (NS - 1)) ^ sel
    pos = (rel_s * N_GRP + rel_g) * NQ + ((src >> 5) & (NQ - 1))
    pair = pair_ref[...] + n_pair * par_ref[...]
    for value, out in (
        (pos * (NT * RA) + (src & (RA - 1)), ci_ref),
        ((pair >> 3) * (NT * RA) + (pair & (RA - 1)), wi_ref),
    ):
        chosen = lax.dot_general(
            value.astype(jnp.float32),
            pick,
            (((1,), (1,)), ((), ())),
            precision=HIGH,
            preferred_element_type=jnp.float32,
        )
        out[pl.ds(0, n_exc), :] = (chosen + 0.5).astype(jnp.int32)
        out[pl.ds(n_exc, EPAD - n_exc), :] = jnp.zeros((EPAD - n_exc, LANES), jnp.int32)


def prep_call(place, src, pair, par, n_pair):
    shape = jax.ShapeDtypeStruct((EPAD, LANES), jnp.int32)
    ci, wi = pl.pallas_call(
        functools.partial(prep_kernel, n_pair),
        out_shape=(shape, shape),
        in_specs=[SMEM, VMEM, VMEM, VMEM],
        out_specs=(VMEM, VMEM),
        name="prep",
    )(place, src, pair, par)
    return tuple(
        pltpu.with_memory_space_constraint(v.reshape(-1), pltpu.HBM) for v in (ci, wi)
    )


def mixed_kernel(n_exc, cidx_hbm, widx_hbm, w_ref, mix_ref, *rest):
    count = N_GRP * NS
    parts = rest[:count]
    o_ref, table, cidx, widx, idx_sem = rest[count:]
    chunks = EPAD // CHUNK
    length = CHUNK * LANES

    def index_copies(k):
        at = pl.ds(k * length, length)
        return (
            pltpu.make_async_copy(cidx_hbm.at[at], cidx.at[at], idx_sem.at[0, k]),
            pltpu.make_async_copy(widx_hbm.at[at], widx.at[at], idx_sem.at[1, k]),
        )

    for k in range(chunks):
        for copy in index_copies(k):
            copy.start()
    for i, part in enumerate(parts):
        table[pl.ds(i * PART, PART), :] = part[...]
    size = (NQ - 1) * RA + 1

    for k in range(chunks):
        for copy in index_copies(k):
            copy.wait()

        def block(q, carry, k=k):
            start = q * RA
            for a in range(RA):
                rows = pl.ds(q * (NT * RA) + a, NT, stride=RA)
                acc = None if k == 0 else o_ref[rows, :]
                for e in range(k * CHUNK, min((k + 1) * CHUNK, n_exc)):
                    base = e * LANES + a
                    ci = cidx.at[pl.ds(base, size)][start]
                    wi = widx.at[pl.ds(base, size)][start]
                    term = (
                        table[pl.ds(ci, NT, stride=RA), :]
                        * w_ref[pl.ds(wi, NT, stride=RA), :]
                    )
                    acc = term if acc is None else acc + term
                o_ref[rows, :] = acc
            if k == 0:
                mix = mix_ref[q, NT][:, : N_GRP * RA]
                for t in range(NT):
                    at = q * (NT * RA) + t * RA
                    stacked = [
                        table[pl.ds(pl.multiple_of(at + h * PART, RA), RA), :]
                        for h in range(N_GRP)
                    ]
                    alpha = jnp.dot(
                        mix,
                        jnp.concatenate(stacked, axis=0),
                        precision=HIGH,
                        preferred_element_type=jnp.float32,
                    )
                    target = pl.ds(pl.multiple_of(at, RA), RA)
                    o_ref[target, :] = o_ref[target, :] + alpha
            return carry

        lax.fori_loop(0, NQ, block, 0)


def mixed_call(cidx, widx, wtab, mix, parts, n_exc):
    count = N_GRP * NS
    index = pltpu.SMEM((EPAD * LANES,), jnp.int32)
    return pl.pallas_call(
        functools.partial(mixed_kernel, n_exc),
        out_shape=jax.ShapeDtypeStruct((PART, LANES), jnp.float32),
        in_specs=[HBM, HBM, VMEM, VMEM] + [VMEM] * count,
        out_specs=VMEM,
        scratch_shapes=[
            pltpu.VMEM((count * PART, LANES), jnp.float32),
            index,
            index,
            pltpu.SemaphoreType.DMA((2, EPAD // CHUNK)),
        ],
        compiler_params=pltpu.CompilerParams(vmem_limit_bytes=16 << 20),
        cost_estimate=pl.CostEstimate(
            flops=n_exc * NQ * RA * NT * LANES * 2,
            bytes_accessed=8 << 20,
            transcendentals=0,
        ),
        name="mixed",
    )(cidx, widx, wtab, mix, *parts)


def per_device(
    coeff,
    beta_blocks,
    block_list,
    alpha_blocks,
    partner_mask,
    exc_source,
    exc_pair,
    exc_parity,
    occupation,
    coulomb,
):
    g = lax.axis_index("grp")
    xl = lax.axis_index("xl")
    c = lax.axis_index("c")
    alpha_rows, beta_width = coeff.shape
    n_exc = exc_source.shape[0]
    n_pair = coulomb.shape[0]

    def shift(value, k):
        return lax.ppermute(
            value, "grp", [(i, (i - k) % N_GRP) for i in range(N_GRP)]
        )

    def swap(value, axis):
        return lax.ppermute(value, axis, [(0, 1), (1, 0)])

    packed = pack(g.reshape(1), partner_mask, coeff, alpha_blocks)
    arrived = lax.all_to_all(
        packed, ("z", "xh"), split_axis=0, concat_axis=0, tiled=True
    )

    sel = xl * NC + c
    place = jnp.stack([g, sel]).astype(jnp.int32)
    cidx, widx = prep_call(place, exc_source, exc_pair, exc_parity, n_pair)
    pieces = [
        lax.ppermute(occupation, ("xl", "c"), [(i, i ^ k) for i in range(NS)])
        for k in range(1, NS)
    ]
    pieces = jnp.stack([occupation] + pieces)
    ordered = [
        lax.dynamic_index_in_dim(pieces, sel ^ k, 0, keepdims=False) for k in range(NS)
    ]
    occ = jnp.concatenate(ordered, axis=1).astype(jnp.float32)
    weights = jnp.dot(coulomb, occ, precision=HIGH, preferred_element_type=jnp.float32)
    signed = jnp.concatenate([weights, -weights], axis=0)
    wtab = (
        signed.reshape(2 * n_pair // RA, RA, NT, LANES)
        .transpose(0, 2, 1, 3)
        .reshape(2 * n_pair * NT, LANES)
    )

    block_size = beta_blocks.shape[1]
    block_count = beta_width // block_size
    blocked = coeff.reshape(alpha_rows, block_count, block_size)
    block_ids = jnp.arange(block_count, dtype=jnp.int32)
    choosing = (block_list[0][:, None] == block_ids[None, :]).astype(jnp.float32)
    picked = jnp.einsum("rnk,pn->rpk", blocked, choosing, precision=HIGH)
    arrived, wtab, cidx, widx, picked = lax.optimization_barrier(
        (arrived, wtab, cidx, widx, picked)
    )
    own = arrived[:, :NT].reshape(PART, LANES)
    after, before = shift(own, 1), shift(own, N_GRP - 1)
    over = swap(own, "xl")
    again, over, after, before = lax.optimization_barrier((own, over, after, before))
    over_after, over_before = swap(after, "xl"), swap(before, "xl")
    two, over_two = shift(again, 2), shift(over, 2)
    (start, after, before, over), over_after = lax.optimization_barrier(
        ((again, after, before, over), over_after)
    )
    near = [start, after, two, before]
    across = [over, over_after, over_two, over_before]
    parts = (
        near
        + [swap(v, "c") for v in near]
        + across
        + [swap(v, "c") for v in across]
    )
    mixed_local = mixed_call(
        cidx,
        widx,
        wtab,
        arrived,
        parts,
        n_exc,
    )
    mixed = lax.all_to_all(
        mixed_local.reshape(NQ, NT, RA, LANES),
        ("z", "xh"),
        split_axis=0,
        concat_axis=0,
        tiled=True,
    )
    mixed = (
        mixed.reshape(NQ * NT, RA, LANES).transpose(1, 0, 2).reshape(alpha_rows, -1)
    )

    applied = jnp.einsum("rpk,pkl->rpl", picked, beta_blocks, precision=HIGH)
    placing = (block_list[1][:, None] == block_ids[None, :]).astype(jnp.float32)
    same_beta = jnp.einsum("rpl,pn->rnl", applied, placing, precision=HIGH).reshape(
        alpha_rows, beta_width
    )

    return mixed + same_beta


def solution(mesh):
    wide = ("z", "xh", "xl", "c")
    fine = Mesh(mesh.devices.reshape(N_GRP, NZ, NXH, NXL, NC), ("grp",) + wide)
    every = ("grp",) + wide
    in_specs = (
        P(every, None),
        P(),
        P(),
        P(every, None, None, None),
        P(every, None),
        P(None, "grp"),
        P(None, "grp"),
        P(None, "grp"),
        P(None, wide),
        P(),
    )
    return jax.shard_map(
        per_device,
        mesh=fine,
        in_specs=in_specs,
        out_specs=P(every, None),
        check_vma=False,
    )
```

```python
import functools

import jax
import jax.numpy as jnp
from jax import lax
from jax.experimental import pallas as pl
from jax.experimental.pallas import tpu as pltpu
from jax.sharding import Mesh
from jax.sharding import PartitionSpec as P

HIGH = lax.Precision.HIGHEST
RA = 8
LANES = 128
N_GRP = 4
NZ, NXH, NXL, NC = 8, 2, 2, 2
NQ = NZ * NXH
NS = NXL * NC
NT = 3
PART = NQ * NT * RA
EPAD = 96
CHUNK = 32

SMEM = pl.BlockSpec(memory_space=pltpu.SMEM)
VMEM = pl.BlockSpec(memory_space=pltpu.VMEM)
HBM = pl.BlockSpec(memory_space=pltpu.HBM)


def pack_kernel(g_ref, mask_ref, x_ref, alpha_ref, o_ref):
    pieces = []
    for rel in range(N_GRP):
        h = (g_ref[0] + rel) & (N_GRP - 1)
        pieces.append(alpha_ref[0, h] * mask_ref[0, h].astype(jnp.float32))
    pieces.append(jnp.zeros((RA, LANES - N_GRP * RA), jnp.float32))
    coupling = jnp.concatenate(pieces, axis=1)
    for j in range(NQ):
        for t in range(NT):
            lo = (j * NT + t) * LANES
            o_ref[j, t] = x_ref[:, lo : lo + LANES]
        o_ref[j, NT] = coupling


def pack(group, mask, coeff, alpha_blocks):
    return pl.pallas_call(
        pack_kernel,
        out_shape=jax.ShapeDtypeStruct((NQ, NT + 1, RA, LANES), jnp.float32),
        in_specs=[SMEM, SMEM, VMEM, VMEM],
        out_specs=VMEM,
        name="pack",
    )(group, mask, coeff, alpha_blocks)


def prep_kernel(n_pair, place_ref, src_ref, pair_ref, par_ref, ci_ref, wi_ref):
    g, sel = place_ref[0], place_ref[1]
    n_exc, row_count = src_ref.shape
    row = lax.broadcasted_iota(jnp.int32, (LANES, row_count), 0)
    col = lax.broadcasted_iota(jnp.int32, (LANES, row_count), 1)
    want = (row >> 3) * (NS * RA) + sel * RA + (row & (RA - 1))
    pick = jnp.where(col == want, 1.0, 0.0)
    src = src_ref[...]
    rel_g = ((src >> 9) - g) & (N_GRP - 1)
    rel_s = ((src >> 3) & (NS - 1)) ^ sel
    pos = (rel_s * N_GRP + rel_g) * NQ + ((src >> 5) & (NQ - 1))
    pair = pair_ref[...] + n_pair * par_ref[...]
    for value, out in (
        (pos * (NT * RA) + (src & (RA - 1)), ci_ref),
        ((pair >> 3) * (NT * RA) + (pair & (RA - 1)), wi_ref),
    ):
        chosen = lax.dot_general(
            value.astype(jnp.float32),
            pick,
            (((1,), (1,)), ((), ())),
            precision=HIGH,
            preferred_element_type=jnp.float32,
        )
        out[pl.ds(0, n_exc), :] = (chosen + 0.5).astype(jnp.int32)
        out[pl.ds(n_exc, EPAD - n_exc), :] = jnp.zeros((EPAD - n_exc, LANES), jnp.int32)


def prep_call(place, src, pair, par, n_pair):
    shape = jax.ShapeDtypeStruct((EPAD, LANES), jnp.int32)
    ci, wi = pl.pallas_call(
        functools.partial(prep_kernel, n_pair),
        out_shape=(shape, shape),
        in_specs=[SMEM, VMEM, VMEM, VMEM],
        out_specs=(VMEM, VMEM),
        name="prep",
    )(place, src, pair, par)
    return tuple(
        pltpu.with_memory_space_constraint(v.reshape(-1), pltpu.HBM) for v in (ci, wi)
    )


def mixed_kernel(n_exc, cidx_hbm, widx_hbm, w_ref, mix_ref, *rest):
    count = N_GRP * NS
    parts = rest[:count]
    o_ref, table, cidx, widx, idx_sem = rest[count:]
    chunks = EPAD // CHUNK
    length = CHUNK * LANES

    def index_copies(k):
        at = pl.ds(k * length, length)
        return (
            pltpu.make_async_copy(cidx_hbm.at[at], cidx.at[at], idx_sem.at[0, k]),
            pltpu.make_async_copy(widx_hbm.at[at], widx.at[at], idx_sem.at[1, k]),
        )

    for k in range(chunks):
        for copy in index_copies(k):
            copy.start()
    for i, part in enumerate(parts):
        table[pl.ds(i * PART, PART), :] = part[...]
    size = (NQ - 1) * RA + 1

    for k in range(chunks):
        for copy in index_copies(k):
            copy.wait()

        def block(q, carry, k=k):
            start = q * RA
            for a in range(RA):
                rows = pl.ds(q * (NT * RA) + a, NT, stride=RA)
                acc = None if k == 0 else o_ref[rows, :]
                for e in range(k * CHUNK, min((k + 1) * CHUNK, n_exc)):
                    base = e * LANES + a
                    ci = cidx.at[pl.ds(base, size)][start]
                    wi = widx.at[pl.ds(base, size)][start]
                    term = (
                        table[pl.ds(ci, NT, stride=RA), :]
                        * w_ref[pl.ds(wi, NT, stride=RA), :]
                    )
                    acc = term if acc is None else acc + term
                o_ref[rows, :] = acc
            if k == 0:
                mix = mix_ref[q, NT][:, : N_GRP * RA]
                for t in range(NT):
                    at = q * (NT * RA) + t * RA
                    stacked = [
                        table[pl.ds(pl.multiple_of(at + h * PART, RA), RA), :]
                        for h in range(N_GRP)
                    ]
                    alpha = jnp.dot(
                        mix,
                        jnp.concatenate(stacked, axis=0),
                        precision=HIGH,
                        preferred_element_type=jnp.float32,
                    )
                    target = pl.ds(pl.multiple_of(at, RA), RA)
                    o_ref[target, :] = o_ref[target, :] + alpha
            return carry

        lax.fori_loop(0, NQ, block, 0)


def mixed_call(cidx, widx, wtab, mix, parts, n_exc):
    count = N_GRP * NS
    index = pltpu.SMEM((EPAD * LANES,), jnp.int32)
    return pl.pallas_call(
        functools.partial(mixed_kernel, n_exc),
        out_shape=jax.ShapeDtypeStruct((PART, LANES), jnp.float32),
        in_specs=[HBM, HBM, VMEM, VMEM] + [VMEM] * count,
        out_specs=VMEM,
        scratch_shapes=[
            pltpu.VMEM((count * PART, LANES), jnp.float32),
            index,
            index,
            pltpu.SemaphoreType.DMA((2, EPAD // CHUNK)),
        ],
        compiler_params=pltpu.CompilerParams(vmem_limit_bytes=16 << 20),
        cost_estimate=pl.CostEstimate(
            flops=n_exc * NQ * RA * NT * LANES * 2,
            bytes_accessed=8 << 20,
            transcendentals=0,
        ),
        name="mixed",
    )(cidx, widx, wtab, mix, *parts)


def place_kernel(list_ref, applied_ref, o_ref):
    o_ref[...] = jnp.zeros(o_ref.shape, jnp.float32)
    for p in range(applied_ref.shape[0]):
        t = list_ref[1, p]
        o_ref[t] = o_ref[t] + applied_ref[p]


def place_call(block_list, applied, block_count):
    return pl.pallas_call(
        place_kernel,
        out_shape=jax.ShapeDtypeStruct((block_count,) + applied.shape[1:], jnp.float32),
        in_specs=[SMEM, VMEM],
        out_specs=VMEM,
        name="place",
    )(block_list, applied)


def per_device(
    coeff,
    beta_blocks,
    block_list,
    alpha_blocks,
    partner_mask,
    exc_source,
    exc_pair,
    exc_parity,
    occupation,
    coulomb,
):
    g = lax.axis_index("grp")
    xl = lax.axis_index("xl")
    c = lax.axis_index("c")
    alpha_rows, beta_width = coeff.shape
    n_exc = exc_source.shape[0]
    n_pair = coulomb.shape[0]

    def shift(value, k):
        return lax.ppermute(
            value, "grp", [(i, (i - k) % N_GRP) for i in range(N_GRP)]
        )

    def swap(value, axis):
        return lax.ppermute(value, axis, [(0, 1), (1, 0)])

    packed = pack(g.reshape(1), partner_mask, coeff, alpha_blocks)
    arrived = lax.all_to_all(
        packed, ("z", "xh"), split_axis=0, concat_axis=0, tiled=True
    )

    sel = xl * NC + c
    place = jnp.stack([g, sel]).astype(jnp.int32)
    cidx, widx = prep_call(place, exc_source, exc_pair, exc_parity, n_pair)
    pieces = [
        lax.ppermute(occupation, ("xl", "c"), [(i, i ^ k) for i in range(NS)])
        for k in range(1, NS)
    ]
    pieces = jnp.stack([occupation] + pieces)
    ordered = [
        lax.dynamic_index_in_dim(pieces, sel ^ k, 0, keepdims=False) for k in range(NS)
    ]
    occ = jnp.concatenate(ordered, axis=1).astype(jnp.float32)
    weights = jnp.dot(coulomb, occ, precision=HIGH, preferred_element_type=jnp.float32)
    signed = jnp.concatenate([weights, -weights], axis=0)
    wtab = (
        signed.reshape(2 * n_pair // RA, RA, NT, LANES)
        .transpose(0, 2, 1, 3)
        .reshape(2 * n_pair * NT, LANES)
    )

    block_size = beta_blocks.shape[1]
    block_count = beta_width // block_size
    blocked = coeff.reshape(alpha_rows, block_count, block_size)
    block_ids = jnp.arange(block_count, dtype=jnp.int32)
    choosing = (block_list[0][:, None] == block_ids[None, :]).astype(jnp.float32)
    picked = jnp.einsum("rnk,pn->prk", blocked, choosing, precision=HIGH)
    arrived, wtab, cidx, widx, picked = lax.optimization_barrier(
        (arrived, wtab, cidx, widx, picked)
    )
    own = arrived[:, :NT].reshape(PART, LANES)
    after, before = shift(own, 1), shift(own, N_GRP - 1)
    over = swap(own, "xl")
    again, over, after, before = lax.optimization_barrier((own, over, after, before))
    over_after, over_before = swap(after, "xl"), swap(before, "xl")
    two, over_two = shift(again, 2), shift(over, 2)
    (start, after, before, over), two = lax.optimization_barrier(
        ((again, after, before, over), two)
    )
    near = [start, after, two, before]
    across = [over, over_after, over_two, over_before]
    parts = (
        near
        + [swap(v, "c") for v in near]
        + across
        + [swap(v, "c") for v in across]
    )
    mixed_local = mixed_call(
        cidx,
        widx,
        wtab,
        arrived,
        parts,
        n_exc,
    )
    mixed = lax.all_to_all(
        mixed_local.reshape(NQ, NT, RA, LANES),
        ("z", "xh"),
        split_axis=0,
        concat_axis=0,
        tiled=True,
    )
    mixed = mixed.reshape(block_count, alpha_rows, block_size)

    applied = jnp.einsum("prk,pkl->prl", picked, beta_blocks, precision=HIGH)
    same_beta = place_call(block_list, applied, block_count)
    total = mixed + same_beta
    return total.transpose(1, 0, 2).reshape(alpha_rows, beta_width)


def solution(mesh):
    wide = ("z", "xh", "xl", "c")
    fine = Mesh(mesh.devices.reshape(N_GRP, NZ, NXH, NXL, NC), ("grp",) + wide)
    every = ("grp",) + wide
    in_specs = (
        P(every, None),
        P(),
        P(),
        P(every, None, None, None),
        P(every, None),
        P(None, "grp"),
        P(None, "grp"),
        P(None, "grp"),
        P(None, wide),
        P(),
    )
    return jax.shard_map(
        per_device,
        mesh=fine,
        in_specs=in_specs,
        out_specs=P(every, None),
        check_vma=False,
    )
```

```python
import functools

import jax
import jax.numpy as jnp
from jax import lax
from jax.experimental import pallas as pl
from jax.experimental.pallas import tpu as pltpu
from jax.sharding import Mesh
from jax.sharding import PartitionSpec as P

HIGH = lax.Precision.HIGHEST
RA = 8
LANES = 128
N_GRP = 4
NZ, NXH, NXL, NC = 8, 2, 2, 2
NQ = NZ * NXH
NS = NXL * NC
NT = 3
PART = NQ * NT * RA
EPAD = 96
PLACES = [(i,) for i in (0, 1, 2, 3, 8, 9, 10, 11, 6, 13, 14, 15)] + [(4, 5, 7, 12)]
CHUNK = 32

SMEM = pl.BlockSpec(memory_space=pltpu.SMEM)
VMEM = pl.BlockSpec(memory_space=pltpu.VMEM)
HBM = pl.BlockSpec(memory_space=pltpu.HBM)


def pack_kernel(g_ref, mask_ref, x_ref, alpha_ref, o_ref):
    pieces = []
    for rel in range(N_GRP):
        h = (g_ref[0] + rel) & (N_GRP - 1)
        pieces.append(alpha_ref[0, h] * mask_ref[0, h].astype(jnp.float32))
    pieces.append(jnp.zeros((RA, LANES - N_GRP * RA), jnp.float32))
    coupling = jnp.concatenate(pieces, axis=1)
    for j in range(NQ):
        for t in range(NT):
            lo = (j * NT + t) * LANES
            o_ref[j, t] = x_ref[:, lo : lo + LANES]
        o_ref[j, NT] = coupling


def pack(group, mask, coeff, alpha_blocks):
    return pl.pallas_call(
        pack_kernel,
        out_shape=jax.ShapeDtypeStruct((NQ, NT + 1, RA, LANES), jnp.float32),
        in_specs=[SMEM, SMEM, VMEM, VMEM],
        out_specs=VMEM,
        name="pack",
    )(group, mask, coeff, alpha_blocks)


def prep_kernel(n_pair, place_ref, src_ref, pair_ref, par_ref, ci_ref, wi_ref):
    g, sel = place_ref[0], place_ref[1]
    n_exc, row_count = src_ref.shape
    row = lax.broadcasted_iota(jnp.int32, (LANES, row_count), 0)
    col = lax.broadcasted_iota(jnp.int32, (LANES, row_count), 1)
    want = (row >> 3) * (NS * RA) + sel * RA + (row & (RA - 1))
    pick = jnp.where(col == want, 1.0, 0.0)
    src = src_ref[...]
    rel_g = ((src >> 9) - g) & (N_GRP - 1)
    rel_s = ((src >> 3) & (NS - 1)) ^ sel
    pos = (rel_s * N_GRP + rel_g) * NQ + ((src >> 5) & (NQ - 1))
    pair = pair_ref[...] + n_pair * par_ref[...]
    for value, out in (
        (pos * (NT * RA) + (src & (RA - 1)), ci_ref),
        ((pair >> 3) * (NT * RA) + (pair & (RA - 1)), wi_ref),
    ):
        chosen = lax.dot_general(
            value.astype(jnp.float32),
            pick,
            (((1,), (1,)), ((), ())),
            precision=HIGH,
            preferred_element_type=jnp.float32,
        )
        out[pl.ds(0, n_exc), :] = (chosen + 0.5).astype(jnp.int32)
        out[pl.ds(n_exc, EPAD - n_exc), :] = jnp.zeros((EPAD - n_exc, LANES), jnp.int32)


def prep_call(place, src, pair, par, n_pair):
    shape = jax.ShapeDtypeStruct((EPAD, LANES), jnp.int32)
    ci, wi = pl.pallas_call(
        functools.partial(prep_kernel, n_pair),
        out_shape=(shape, shape),
        in_specs=[SMEM, VMEM, VMEM, VMEM],
        out_specs=(VMEM, VMEM),
        name="prep",
    )(place, src, pair, par)
    return tuple(
        pltpu.with_memory_space_constraint(v.reshape(-1), pltpu.HBM) for v in (ci, wi)
    )


def mixed_kernel(n_exc, cidx_hbm, widx_hbm, w_ref, mix_ref, *rest):
    count = len(PLACES)
    parts = rest[:count]
    o_ref, table, cidx, widx, idx_sem = rest[count:]
    chunks = EPAD // CHUNK
    length = CHUNK * LANES

    def index_copies(k):
        at = pl.ds(k * length, length)
        return (
            pltpu.make_async_copy(cidx_hbm.at[at], cidx.at[at], idx_sem.at[0, k]),
            pltpu.make_async_copy(widx_hbm.at[at], widx.at[at], idx_sem.at[1, k]),
        )

    for k in range(chunks):
        for copy in index_copies(k):
            copy.start()
    for part, slots in zip(parts, PLACES):
        for i, slot in enumerate(slots):
            table[pl.ds(slot * PART, PART), :] = part[pl.ds(i * PART, PART), :]
    size = (NQ - 1) * RA + 1

    for k in range(chunks):
        for copy in index_copies(k):
            copy.wait()

        def block(q, carry, k=k):
            start = q * RA
            for a in range(RA):
                rows = pl.ds(q * (NT * RA) + a, NT, stride=RA)
                acc = None if k == 0 else o_ref[rows, :]
                for e in range(k * CHUNK, min((k + 1) * CHUNK, n_exc)):
                    base = e * LANES + a
                    ci = cidx.at[pl.ds(base, size)][start]
                    wi = widx.at[pl.ds(base, size)][start]
                    term = (
                        table[pl.ds(ci, NT, stride=RA), :]
                        * w_ref[pl.ds(wi, NT, stride=RA), :]
                    )
                    acc = term if acc is None else acc + term
                o_ref[rows, :] = acc
            if k == 0:
                mix = mix_ref[q, NT][:, : N_GRP * RA]
                for t in range(NT):
                    at = q * (NT * RA) + t * RA
                    stacked = [
                        table[pl.ds(pl.multiple_of(at + h * PART, RA), RA), :]
                        for h in range(N_GRP)
                    ]
                    alpha = jnp.dot(
                        mix,
                        jnp.concatenate(stacked, axis=0),
                        precision=HIGH,
                        preferred_element_type=jnp.float32,
                    )
                    target = pl.ds(pl.multiple_of(at, RA), RA)
                    o_ref[target, :] = o_ref[target, :] + alpha
            return carry

        lax.fori_loop(0, NQ, block, 0)


def mixed_call(cidx, widx, wtab, mix, parts, n_exc):
    count = N_GRP * NS
    index = pltpu.SMEM((EPAD * LANES,), jnp.int32)
    return pl.pallas_call(
        functools.partial(mixed_kernel, n_exc),
        out_shape=jax.ShapeDtypeStruct((PART, LANES), jnp.float32),
        in_specs=[HBM, HBM, VMEM, VMEM] + [VMEM] * len(parts),
        out_specs=VMEM,
        scratch_shapes=[
            pltpu.VMEM((count * PART, LANES), jnp.float32),
            index,
            index,
            pltpu.SemaphoreType.DMA((2, EPAD // CHUNK)),
        ],
        compiler_params=pltpu.CompilerParams(vmem_limit_bytes=16 << 20),
        cost_estimate=pl.CostEstimate(
            flops=n_exc * NQ * RA * NT * LANES * 2,
            bytes_accessed=8 << 20,
            transcendentals=0,
        ),
        name="mixed",
    )(cidx, widx, wtab, mix, *parts)


def per_device(
    coeff,
    beta_blocks,
    block_list,
    alpha_blocks,
    partner_mask,
    exc_source,
    exc_pair,
    exc_parity,
    occupation,
    coulomb,
):
    g = lax.axis_index("grp")
    xl = lax.axis_index("xl")
    c = lax.axis_index("c")
    alpha_rows, beta_width = coeff.shape
    n_exc = exc_source.shape[0]
    n_pair = coulomb.shape[0]

    def shift(value, k):
        return lax.ppermute(
            value, "grp", [(i, (i - k) % N_GRP) for i in range(N_GRP)]
        )

    def swap(value, axis):
        return lax.ppermute(value, axis, [(0, 1), (1, 0)])

    packed = pack(g.reshape(1), partner_mask, coeff, alpha_blocks)
    arrived = lax.all_to_all(
        packed, ("z", "xh"), split_axis=0, concat_axis=0, tiled=True
    )

    sel = xl * NC + c
    place = jnp.stack([g, sel]).astype(jnp.int32)
    cidx, widx = prep_call(place, exc_source, exc_pair, exc_parity, n_pair)
    pieces = [
        lax.ppermute(occupation, ("xl", "c"), [(i, i ^ k) for i in range(NS)])
        for k in range(1, NS)
    ]
    pieces = jnp.stack([occupation] + pieces)
    ordered = [
        lax.dynamic_index_in_dim(pieces, sel ^ k, 0, keepdims=False) for k in range(NS)
    ]
    occ = jnp.concatenate(ordered, axis=1).astype(jnp.float32)
    weights = jnp.dot(coulomb, occ, precision=HIGH, preferred_element_type=jnp.float32)
    signed = jnp.concatenate([weights, -weights], axis=0)
    wtab = (
        signed.reshape(2 * n_pair // RA, RA, NT, LANES)
        .transpose(0, 2, 1, 3)
        .reshape(2 * n_pair * NT, LANES)
    )

    block_size = beta_blocks.shape[1]
    block_count = beta_width // block_size
    blocked = coeff.reshape(alpha_rows, block_count, block_size)
    block_ids = jnp.arange(block_count, dtype=jnp.int32)
    choosing = (block_list[0][:, None] == block_ids[None, :]).astype(jnp.float32)
    picked = jnp.einsum("rnk,pn->rpk", blocked, choosing, precision=HIGH)
    arrived, wtab, cidx, widx, picked = lax.optimization_barrier(
        (arrived, wtab, cidx, widx, picked)
    )
    own = arrived[:, :NT].reshape(PART, LANES)
    after, before = shift(own, 1), shift(own, N_GRP - 1)
    over = swap(own, "xl")
    again, over, after, before = lax.optimization_barrier((own, over, after, before))
    over_after, over_before = swap(after, "xl"), swap(before, "xl")
    two, over_two = shift(again, 2), shift(over, 2)
    joined = swap(jnp.concatenate([again, after, before, over], axis=0), "c")
    near = [again, after, two, before]
    across = [over, over_after, over_two, over_before]
    late = [swap(v, "c") for v in (two, over_after, over_two, over_before)]
    parts = near + across + late + [joined]
    mixed_local = mixed_call(
        cidx,
        widx,
        wtab,
        arrived,
        parts,
        n_exc,
    )
    mixed = lax.all_to_all(
        mixed_local.reshape(NQ, NT, RA, LANES),
        ("z", "xh"),
        split_axis=0,
        concat_axis=0,
        tiled=True,
    )
    mixed = (
        mixed.reshape(NQ * NT, RA, LANES).transpose(1, 0, 2).reshape(alpha_rows, -1)
    )

    applied = jnp.einsum("rpk,pkl->rpl", picked, beta_blocks, precision=HIGH)
    placing = (block_list[1][:, None] == block_ids[None, :]).astype(jnp.float32)
    same_beta = jnp.einsum("rpl,pn->rnl", applied, placing, precision=HIGH).reshape(
        alpha_rows, beta_width
    )

    return mixed + same_beta


def solution(mesh):
    wide = ("z", "xh", "xl", "c")
    fine = Mesh(mesh.devices.reshape(N_GRP, NZ, NXH, NXL, NC), ("grp",) + wide)
    every = ("grp",) + wide
    in_specs = (
        P(every, None),
        P(),
        P(),
        P(every, None, None, None),
        P(every, None),
        P(None, "grp"),
        P(None, "grp"),
        P(None, "grp"),
        P(None, wide),
        P(),
    )
    return jax.shard_map(
        per_device,
        mesh=fine,
        in_specs=in_specs,
        out_specs=P(every, None),
        check_vma=False,
    )
```

```python
import functools

import jax
import jax.numpy as jnp
from jax import lax
from jax.experimental import pallas as pl
from jax.experimental.pallas import tpu as pltpu
from jax.sharding import Mesh
from jax.sharding import PartitionSpec as P

HIGH = lax.Precision.HIGHEST
RA = 8
LANES = 128
N_GRP = 4
NZ, NXH, NXL, NC = 8, 2, 2, 2
NQ = NZ * NXH
NS = NXL * NC
NT = 3
PART = NQ * NT * RA
EPAD = 96
CHUNK = 32

SMEM = pl.BlockSpec(memory_space=pltpu.SMEM)
VMEM = pl.BlockSpec(memory_space=pltpu.VMEM)
HBM = pl.BlockSpec(memory_space=pltpu.HBM)


def pack_kernel(g_ref, mask_ref, x_ref, alpha_ref, o_ref):
    pieces = []
    for rel in range(N_GRP):
        h = (g_ref[0] + rel) & (N_GRP - 1)
        pieces.append(alpha_ref[0, h] * mask_ref[0, h].astype(jnp.float32))
    pieces.append(jnp.zeros((RA, LANES - N_GRP * RA), jnp.float32))
    coupling = jnp.concatenate(pieces, axis=1)
    for j in range(NQ):
        for t in range(NT):
            lo = (j * NT + t) * LANES
            o_ref[j, t] = x_ref[:, lo : lo + LANES]
        o_ref[j, NT] = coupling


def pack(group, mask, coeff, alpha_blocks):
    return pl.pallas_call(
        pack_kernel,
        out_shape=jax.ShapeDtypeStruct((NQ, NT + 1, RA, LANES), jnp.float32),
        in_specs=[SMEM, SMEM, VMEM, VMEM],
        out_specs=VMEM,
        name="pack",
    )(group, mask, coeff, alpha_blocks)


def prep_kernel(n_pair, place_ref, src_ref, pair_ref, par_ref, ci_ref, wi_ref):
    g, sel = place_ref[0], place_ref[1]
    n_exc, row_count = src_ref.shape
    row = lax.broadcasted_iota(jnp.int32, (LANES, row_count), 0)
    col = lax.broadcasted_iota(jnp.int32, (LANES, row_count), 1)
    want = (row >> 3) * (NS * RA) + sel * RA + (row & (RA - 1))
    pick = jnp.where(col == want, 1.0, 0.0)
    src = src_ref[...]
    rel_g = ((src >> 9) - g) & (N_GRP - 1)
    rel_s = ((src >> 3) & (NS - 1)) ^ sel
    pos = (rel_s * N_GRP + rel_g) * NQ + ((src >> 5) & (NQ - 1))
    pair = pair_ref[...] + n_pair * par_ref[...]
    for value, out in (
        (pos * (NT * RA) + (src & (RA - 1)), ci_ref),
        ((pair >> 3) * (NT * RA) + (pair & (RA - 1)), wi_ref),
    ):
        chosen = lax.dot_general(
            value.astype(jnp.float32),
            pick,
            (((1,), (1,)), ((), ())),
            precision=HIGH,
            preferred_element_type=jnp.float32,
        )
        out[pl.ds(0, n_exc), :] = (chosen + 0.5).astype(jnp.int32)
        out[pl.ds(n_exc, EPAD - n_exc), :] = jnp.zeros((EPAD - n_exc, LANES), jnp.int32)


def prep_call(place, src, pair, par, n_pair):
    shape = jax.ShapeDtypeStruct((EPAD, LANES), jnp.int32)
    ci, wi = pl.pallas_call(
        functools.partial(prep_kernel, n_pair),
        out_shape=(shape, shape),
        in_specs=[SMEM, VMEM, VMEM, VMEM],
        out_specs=(VMEM, VMEM),
        name="prep",
    )(place, src, pair, par)
    return tuple(
        pltpu.with_memory_space_constraint(v.reshape(-1), pltpu.HBM) for v in (ci, wi)
    )


def mixed_kernel(n_exc, cidx_hbm, widx_hbm, w_ref, mix_ref, *rest):
    count = N_GRP * NS
    parts = rest[:count]
    o_ref, table, cidx, widx, idx_sem = rest[count:]
    chunks = EPAD // CHUNK
    length = CHUNK * LANES

    def index_copies(k):
        at = pl.ds(k * length, length)
        return (
            pltpu.make_async_copy(cidx_hbm.at[at], cidx.at[at], idx_sem.at[0, k]),
            pltpu.make_async_copy(widx_hbm.at[at], widx.at[at], idx_sem.at[1, k]),
        )

    for k in range(chunks):
        for copy in index_copies(k):
            copy.start()
    for i, part in enumerate(parts):
        table[pl.ds(i * PART, PART), :] = part[...]
    size = (NQ - 1) * RA + 1

    for k in range(chunks):
        for copy in index_copies(k):
            copy.wait()

        def block(q, carry, k=k):
            start = q * RA
            for a in range(RA):
                rows = pl.ds(q * (NT * RA) + a, NT, stride=RA)
                acc = None if k == 0 else o_ref[rows, :]
                for e in range(k * CHUNK, min((k + 1) * CHUNK, n_exc)):
                    base = e * LANES + a
                    ci = cidx.at[pl.ds(base, size)][start]
                    wi = widx.at[pl.ds(base, size)][start]
                    term = (
                        table[pl.ds(ci, NT, stride=RA), :]
                        * w_ref[pl.ds(wi, NT, stride=RA), :]
                    )
                    acc = term if acc is None else acc + term
                o_ref[rows, :] = acc
            if k == 0:
                mix = mix_ref[q, NT][:, : N_GRP * RA]
                for t in range(NT):
                    at = q * (NT * RA) + t * RA
                    stacked = [
                        table[pl.ds(pl.multiple_of(at + h * PART, RA), RA), :]
                        for h in range(N_GRP)
                    ]
                    alpha = jnp.dot(
                        mix,
                        jnp.concatenate(stacked, axis=0),
                        precision=HIGH,
                        preferred_element_type=jnp.float32,
                    )
                    target = pl.ds(pl.multiple_of(at, RA), RA)
                    o_ref[target, :] = o_ref[target, :] + alpha
            return carry

        lax.fori_loop(0, NQ, block, 0)


def mixed_call(cidx, widx, wtab, mix, parts, n_exc):
    count = N_GRP * NS
    index = pltpu.SMEM((EPAD * LANES,), jnp.int32)
    return pl.pallas_call(
        functools.partial(mixed_kernel, n_exc),
        out_shape=jax.ShapeDtypeStruct((PART, LANES), jnp.float32),
        in_specs=[HBM, HBM, VMEM, VMEM] + [VMEM] * count,
        out_specs=VMEM,
        scratch_shapes=[
            pltpu.VMEM((count * PART, LANES), jnp.float32),
            index,
            index,
            pltpu.SemaphoreType.DMA((2, EPAD // CHUNK)),
        ],
        compiler_params=pltpu.CompilerParams(vmem_limit_bytes=16 << 20),
        cost_estimate=pl.CostEstimate(
            flops=n_exc * NQ * RA * NT * LANES * 2,
            bytes_accessed=8 << 20,
            transcendentals=0,
        ),
        name="mixed",
    )(cidx, widx, wtab, mix, *parts)


def weights_table(pieces, coulomb, sel):
    n_pair = coulomb.shape[0]
    pieces = jnp.stack(pieces)
    ordered = [
        lax.dynamic_index_in_dim(pieces, sel ^ k, 0, keepdims=False) for k in range(NS)
    ]
    occ = jnp.concatenate(ordered, axis=1).astype(jnp.float32)
    weights = jnp.dot(coulomb, occ, precision=HIGH, preferred_element_type=jnp.float32)
    signed = jnp.concatenate([weights, -weights], axis=0)
    return (
        signed.reshape(2 * n_pair // RA, RA, NT, LANES)
        .transpose(0, 2, 1, 3)
        .reshape(2 * n_pair * NT, LANES)
    )


def per_device(
    coeff,
    beta_blocks,
    block_list,
    alpha_blocks,
    partner_mask,
    exc_source,
    exc_pair,
    exc_parity,
    occupation,
    coulomb,
):
    g = lax.axis_index("grp")
    xl = lax.axis_index("xl")
    c = lax.axis_index("c")
    alpha_rows, beta_width = coeff.shape
    n_exc = exc_source.shape[0]
    n_pair = coulomb.shape[0]

    def shift(value, k):
        return lax.ppermute(
            value, "grp", [(i, (i - k) % N_GRP) for i in range(N_GRP)]
        )

    def swap(value, axis):
        return lax.ppermute(value, axis, [(0, 1), (1, 0)])

    packed = pack(g.reshape(1), partner_mask, coeff, alpha_blocks)
    arrived = lax.all_to_all(
        packed, ("z", "xh"), split_axis=0, concat_axis=0, tiled=True
    )

    sel = xl * NC + c
    place = jnp.stack([g, sel]).astype(jnp.int32)
    cidx, widx = prep_call(place, exc_source, exc_pair, exc_parity, n_pair)
    block_size = beta_blocks.shape[1]
    block_count = beta_width // block_size
    blocked = coeff.reshape(alpha_rows, block_count, block_size)
    block_ids = jnp.arange(block_count, dtype=jnp.int32)
    choosing = (block_list[0][:, None] == block_ids[None, :]).astype(jnp.float32)
    picked = jnp.einsum("rnk,pn->rpk", blocked, choosing, precision=HIGH)
    arrived, cidx, widx, picked, occupation = lax.optimization_barrier(
        (arrived, cidx, widx, picked, occupation)
    )
    own = arrived[:, :NT].reshape(PART, LANES)
    after, before = shift(own, 1), shift(own, N_GRP - 1)
    over = swap(own, "xl")
    pieces = [occupation] + [
        lax.ppermute(occupation, ("xl", "c"), [(i, i ^ k) for i in range(NS)])
        for k in range(1, NS)
    ]
    again, over, after, before, pieces = lax.optimization_barrier(
        (own, over, after, before, pieces)
    )
    over_after, over_before = swap(after, "xl"), swap(before, "xl")
    two, over_two = shift(again, 2), shift(over, 2)
    wtab = weights_table(pieces, coulomb, sel)
    (start, after, before, over), over_after, wtab = lax.optimization_barrier(
        ((again, after, before, over), over_after, wtab)
    )
    near = [start, after, two, before]
    across = [over, over_after, over_two, over_before]
    parts = (
        near
        + [swap(v, "c") for v in near]
        + across
        + [swap(v, "c") for v in across]
    )
    mixed_local = mixed_call(
        cidx,
        widx,
        wtab,
        arrived,
        parts,
        n_exc,
    )
    mixed = lax.all_to_all(
        mixed_local.reshape(NQ, NT, RA, LANES),
        ("z", "xh"),
        split_axis=0,
        concat_axis=0,
        tiled=True,
    )
    mixed = (
        mixed.reshape(NQ * NT, RA, LANES).transpose(1, 0, 2).reshape(alpha_rows, -1)
    )

    applied = jnp.einsum("rpk,pkl->rpl", picked, beta_blocks, precision=HIGH)
    placing = (block_list[1][:, None] == block_ids[None, :]).astype(jnp.float32)
    same_beta = jnp.einsum("rpl,pn->rnl", applied, placing, precision=HIGH).reshape(
        alpha_rows, beta_width
    )

    return mixed + same_beta


def solution(mesh):
    wide = ("z", "xh", "xl", "c")
    fine = Mesh(mesh.devices.reshape(N_GRP, NZ, NXH, NXL, NC), ("grp",) + wide)
    every = ("grp",) + wide
    in_specs = (
        P(every, None),
        P(),
        P(),
        P(every, None, None, None),
        P(every, None),
        P(None, "grp"),
        P(None, "grp"),
        P(None, "grp"),
        P(None, wide),
        P(),
    )
    return jax.shard_map(
        per_device,
        mesh=fine,
        in_specs=in_specs,
        out_specs=P(every, None),
        check_vma=False,
    )
```

```python
import functools

import jax
import jax.numpy as jnp
from jax import lax
from jax.experimental import pallas as pl
from jax.experimental.pallas import tpu as pltpu
from jax.sharding import Mesh
from jax.sharding import PartitionSpec as P

HIGH = lax.Precision.HIGHEST
RA = 8
LANES = 128
N_GRP = 4
NZ, NXH, NXL, NC = 8, 2, 2, 2
NQ = NZ * NXH
NS = NXL * NC
NT = 3
PART = NQ * NT * RA
EPAD = 96
BOUNDS = (0, 8, 48, EPAD)

SMEM = pl.BlockSpec(memory_space=pltpu.SMEM)
VMEM = pl.BlockSpec(memory_space=pltpu.VMEM)
HBM = pl.BlockSpec(memory_space=pltpu.HBM)


def pack_kernel(g_ref, mask_ref, x_ref, alpha_ref, o_ref):
    pieces = []
    for rel in range(N_GRP):
        h = (g_ref[0] + rel) & (N_GRP - 1)
        pieces.append(alpha_ref[0, h] * mask_ref[0, h].astype(jnp.float32))
    pieces.append(jnp.zeros((RA, LANES - N_GRP * RA), jnp.float32))
    coupling = jnp.concatenate(pieces, axis=1)
    for j in range(NQ):
        for t in range(NT):
            lo = (j * NT + t) * LANES
            o_ref[j, t] = x_ref[:, lo : lo + LANES]
        o_ref[j, NT] = coupling


def pack(group, mask, coeff, alpha_blocks):
    return pl.pallas_call(
        pack_kernel,
        out_shape=jax.ShapeDtypeStruct((NQ, NT + 1, RA, LANES), jnp.float32),
        in_specs=[SMEM, SMEM, VMEM, VMEM],
        out_specs=VMEM,
        name="pack",
    )(group, mask, coeff, alpha_blocks)


def prep_kernel(n_pair, place_ref, src_ref, pair_ref, par_ref, ci_ref, wi_ref):
    g, sel = place_ref[0], place_ref[1]
    n_exc, row_count = src_ref.shape
    row = lax.broadcasted_iota(jnp.int32, (LANES, row_count), 0)
    col = lax.broadcasted_iota(jnp.int32, (LANES, row_count), 1)
    want = (row >> 3) * (NS * RA) + sel * RA + (row & (RA - 1))
    pick = jnp.where(col == want, 1.0, 0.0)
    src = src_ref[...]
    rel_g = ((src >> 9) - g) & (N_GRP - 1)
    rel_s = ((src >> 3) & (NS - 1)) ^ sel
    pos = (rel_s * N_GRP + rel_g) * NQ + ((src >> 5) & (NQ - 1))
    pair = pair_ref[...] + n_pair * par_ref[...]
    for value, out in (
        (pos * (NT * RA) + (src & (RA - 1)), ci_ref),
        ((pair >> 3) * (NT * RA) + (pair & (RA - 1)), wi_ref),
    ):
        chosen = lax.dot_general(
            value.astype(jnp.float32),
            pick,
            (((1,), (1,)), ((), ())),
            precision=HIGH,
            preferred_element_type=jnp.float32,
        )
        out[pl.ds(0, n_exc), :] = (chosen + 0.5).astype(jnp.int32)
        out[pl.ds(n_exc, EPAD - n_exc), :] = jnp.zeros((EPAD - n_exc, LANES), jnp.int32)


def prep_call(place, src, pair, par, n_pair):
    shape = jax.ShapeDtypeStruct((EPAD, LANES), jnp.int32)
    ci, wi = pl.pallas_call(
        functools.partial(prep_kernel, n_pair),
        out_shape=(shape, shape),
        in_specs=[SMEM, VMEM, VMEM, VMEM],
        out_specs=(VMEM, VMEM),
        name="prep",
    )(place, src, pair, par)
    return tuple(
        pltpu.with_memory_space_constraint(v.reshape(-1), pltpu.HBM) for v in (ci, wi)
    )


def mixed_kernel(n_exc, cidx_hbm, widx_hbm, w_ref, mix_ref, *rest):
    count = N_GRP * NS
    parts = rest[:count]
    o_ref, table, cidx, widx, idx_sem = rest[count:]
    chunks = len(BOUNDS) - 1

    def index_copies(k):
        at = pl.ds(BOUNDS[k] * LANES, (BOUNDS[k + 1] - BOUNDS[k]) * LANES)
        return (
            pltpu.make_async_copy(cidx_hbm.at[at], cidx.at[at], idx_sem.at[0, k]),
            pltpu.make_async_copy(widx_hbm.at[at], widx.at[at], idx_sem.at[1, k]),
        )

    for k in range(chunks):
        for copy in index_copies(k):
            copy.start()
    for i, part in enumerate(parts):
        table[pl.ds(i * PART, PART), :] = part[...]
    size = (NQ - 1) * RA + 1

    for k in range(chunks):
        for copy in index_copies(k):
            copy.wait()

        def block(q, carry, k=k):
            start = q * RA
            for a in range(RA):
                rows = pl.ds(q * (NT * RA) + a, NT, stride=RA)
                acc = None if k == 0 else o_ref[rows, :]
                for e in range(BOUNDS[k], min(BOUNDS[k + 1], n_exc)):
                    base = e * LANES + a
                    ci = cidx.at[pl.ds(base, size)][start]
                    wi = widx.at[pl.ds(base, size)][start]
                    term = (
                        table[pl.ds(ci, NT, stride=RA), :]
                        * w_ref[pl.ds(wi, NT, stride=RA), :]
                    )
                    acc = term if acc is None else acc + term
                o_ref[rows, :] = acc
            if k == 1:
                mix = mix_ref[q, NT][:, : N_GRP * RA]
                for t in range(NT):
                    at = q * (NT * RA) + t * RA
                    stacked = [
                        table[pl.ds(pl.multiple_of(at + h * PART, RA), RA), :]
                        for h in range(N_GRP)
                    ]
                    alpha = jnp.dot(
                        mix,
                        jnp.concatenate(stacked, axis=0),
                        precision=HIGH,
                        preferred_element_type=jnp.float32,
                    )
                    target = pl.ds(pl.multiple_of(at, RA), RA)
                    o_ref[target, :] = o_ref[target, :] + alpha
            return carry

        lax.fori_loop(0, NQ, block, 0)


def mixed_call(cidx, widx, wtab, mix, parts, n_exc):
    count = N_GRP * NS
    index = pltpu.SMEM((EPAD * LANES,), jnp.int32)
    return pl.pallas_call(
        functools.partial(mixed_kernel, n_exc),
        out_shape=jax.ShapeDtypeStruct((PART, LANES), jnp.float32),
        in_specs=[HBM, HBM, VMEM, VMEM] + [VMEM] * count,
        out_specs=VMEM,
        scratch_shapes=[
            pltpu.VMEM((count * PART, LANES), jnp.float32),
            index,
            index,
            pltpu.SemaphoreType.DMA((2, len(BOUNDS) - 1)),
        ],
        compiler_params=pltpu.CompilerParams(vmem_limit_bytes=16 << 20),
        cost_estimate=pl.CostEstimate(
            flops=n_exc * NQ * RA * NT * LANES * 2,
            bytes_accessed=8 << 20,
            transcendentals=0,
        ),
        name="mixed",
    )(cidx, widx, wtab, mix, *parts)


def per_device(
    coeff,
    beta_blocks,
    block_list,
    alpha_blocks,
    partner_mask,
    exc_source,
    exc_pair,
    exc_parity,
    occupation,
    coulomb,
):
    g = lax.axis_index("grp")
    xl = lax.axis_index("xl")
    c = lax.axis_index("c")
    alpha_rows, beta_width = coeff.shape
    n_exc = exc_source.shape[0]
    n_pair = coulomb.shape[0]

    def shift(value, k):
        return lax.ppermute(
            value, "grp", [(i, (i - k) % N_GRP) for i in range(N_GRP)]
        )

    def swap(value, axis):
        return lax.ppermute(value, axis, [(0, 1), (1, 0)])

    packed = pack(g.reshape(1), partner_mask, coeff, alpha_blocks)
    arrived = lax.all_to_all(
        packed, ("z", "xh"), split_axis=0, concat_axis=0, tiled=True
    )

    sel = xl * NC + c
    place = jnp.stack([g, sel]).astype(jnp.int32)
    cidx, widx = prep_call(place, exc_source, exc_pair, exc_parity, n_pair)
    pieces = [
        lax.ppermute(occupation, ("xl", "c"), [(i, i ^ k) for i in range(NS)])
        for k in range(1, NS)
    ]
    pieces = jnp.stack([occupation] + pieces)
    ordered = [
        lax.dynamic_index_in_dim(pieces, sel ^ k, 0, keepdims=False) for k in range(NS)
    ]
    occ = jnp.concatenate(ordered, axis=1).astype(jnp.float32)
    weights = jnp.dot(coulomb, occ, precision=HIGH, preferred_element_type=jnp.float32)
    signed = jnp.concatenate([weights, -weights], axis=0)
    wtab = (
        signed.reshape(2 * n_pair // RA, RA, NT, LANES)
        .transpose(0, 2, 1, 3)
        .reshape(2 * n_pair * NT, LANES)
    )

    block_size = beta_blocks.shape[1]
    block_count = beta_width // block_size
    blocked = coeff.reshape(alpha_rows, block_count, block_size)
    block_ids = jnp.arange(block_count, dtype=jnp.int32)
    choosing = (block_list[0][:, None] == block_ids[None, :]).astype(jnp.float32)
    picked = jnp.einsum("rnk,pn->rpk", blocked, choosing, precision=HIGH)
    arrived, wtab, cidx, widx, picked = lax.optimization_barrier(
        (arrived, wtab, cidx, widx, picked)
    )
    own = arrived[:, :NT].reshape(PART, LANES)
    after, before = shift(own, 1), shift(own, N_GRP - 1)
    over = swap(own, "xl")
    again, over, after, before, twin = lax.optimization_barrier(
        (own, over, after, before, swap(own, "c"))
    )
    over_after, over_before = swap(after, "xl"), swap(before, "xl")
    two, over_two = shift(again, 2), shift(over, 2)
    (after, before, over), over_after = lax.optimization_barrier(
        ((after, before, over), over_after)
    )
    near = [own, after, two, before]
    across = [over, over_after, over_two, over_before]
    parts = (
        near
        + [twin]
        + [swap(v, "c") for v in near[1:]]
        + across
        + [swap(v, "c") for v in across]
    )
    mixed_local = mixed_call(
        cidx,
        widx,
        wtab,
        arrived,
        parts,
        n_exc,
    )
    mixed = lax.all_to_all(
        mixed_local.reshape(NQ, NT, RA, LANES),
        ("z", "xh"),
        split_axis=0,
        concat_axis=0,
        tiled=True,
    )
    mixed = (
        mixed.reshape(NQ * NT, RA, LANES).transpose(1, 0, 2).reshape(alpha_rows, -1)
    )

    applied = jnp.einsum("rpk,pkl->rpl", picked, beta_blocks, precision=HIGH)
    placing = (block_list[1][:, None] == block_ids[None, :]).astype(jnp.float32)
    same_beta = jnp.einsum("rpl,pn->rnl", applied, placing, precision=HIGH).reshape(
        alpha_rows, beta_width
    )

    return mixed + same_beta


def solution(mesh):
    wide = ("z", "xh", "xl", "c")
    fine = Mesh(mesh.devices.reshape(N_GRP, NZ, NXH, NXL, NC), ("grp",) + wide)
    every = ("grp",) + wide
    in_specs = (
        P(every, None),
        P(),
        P(),
        P(every, None, None, None),
        P(every, None),
        P(None, "grp"),
        P(None, "grp"),
        P(None, "grp"),
        P(None, wide),
        P(),
    )
    return jax.shard_map(
        per_device,
        mesh=fine,
        in_specs=in_specs,
        out_specs=P(every, None),
        check_vma=False,
    )
```

```python
import functools

import jax
import jax.numpy as jnp
from jax import lax
from jax.experimental import pallas as pl
from jax.experimental.pallas import tpu as pltpu
from jax.sharding import Mesh
from jax.sharding import PartitionSpec as P

HIGH = lax.Precision.HIGHEST
RA = 8
LANES = 128
N_GRP = 4
NZ, NXH, NXL, NC = 8, 2, 2, 2
NQ = NZ * NXH
NS = NXL * NC
NT = 3
PART = NQ * NT * RA
EPAD = 96
BOUNDS = (0, 8, 48, EPAD)

SMEM = pl.BlockSpec(memory_space=pltpu.SMEM)
VMEM = pl.BlockSpec(memory_space=pltpu.VMEM)
HBM = pl.BlockSpec(memory_space=pltpu.HBM)


def pack_kernel(g_ref, mask_ref, x_ref, alpha_ref, o_ref):
    pieces = []
    for rel in range(N_GRP):
        h = (g_ref[0] + rel) & (N_GRP - 1)
        pieces.append(alpha_ref[0, h] * mask_ref[0, h].astype(jnp.float32))
    pieces.append(jnp.zeros((RA, LANES - N_GRP * RA), jnp.float32))
    coupling = jnp.concatenate(pieces, axis=1)
    for j in range(NQ):
        for t in range(NT):
            lo = (j * NT + t) * LANES
            o_ref[j, t] = x_ref[:, lo : lo + LANES]
        o_ref[j, NT] = coupling


def pack(group, mask, coeff, alpha_blocks):
    return pl.pallas_call(
        pack_kernel,
        out_shape=jax.ShapeDtypeStruct((NQ, NT + 1, RA, LANES), jnp.float32),
        in_specs=[SMEM, SMEM, VMEM, VMEM],
        out_specs=VMEM,
        name="pack",
    )(group, mask, coeff, alpha_blocks)


def prep_kernel(n_pair, place_ref, src_ref, pair_ref, par_ref, ci_ref, wi_ref):
    g, sel = place_ref[0], place_ref[1]
    n_exc, row_count = src_ref.shape
    row = lax.broadcasted_iota(jnp.int32, (LANES, row_count), 0)
    col = lax.broadcasted_iota(jnp.int32, (LANES, row_count), 1)
    want = (row >> 3) * (NS * RA) + sel * RA + (row & (RA - 1))
    pick = jnp.where(col == want, 1.0, 0.0)
    src = src_ref[...]
    rel_g = ((src >> 9) - g) & (N_GRP - 1)
    rel_s = ((src >> 3) & (NS - 1)) ^ sel
    pos = (rel_s * N_GRP + rel_g) * NQ + ((src >> 5) & (NQ - 1))
    pair = pair_ref[...] + n_pair * par_ref[...]
    for value, out in (
        (pos * (NT * RA) + (src & (RA - 1)), ci_ref),
        ((pair >> 3) * (NT * RA) + (pair & (RA - 1)), wi_ref),
    ):
        chosen = lax.dot_general(
            value.astype(jnp.float32),
            pick,
            (((1,), (1,)), ((), ())),
            precision=HIGH,
            preferred_element_type=jnp.float32,
        )
        out[pl.ds(0, n_exc), :] = (chosen + 0.5).astype(jnp.int32)
        out[pl.ds(n_exc, EPAD - n_exc), :] = jnp.zeros((EPAD - n_exc, LANES), jnp.int32)


def prep_call(place, src, pair, par, n_pair):
    shape = jax.ShapeDtypeStruct((EPAD, LANES), jnp.int32)
    ci, wi = pl.pallas_call(
        functools.partial(prep_kernel, n_pair),
        out_shape=(shape, shape),
        in_specs=[SMEM, VMEM, VMEM, VMEM],
        out_specs=(VMEM, VMEM),
        name="prep",
    )(place, src, pair, par)
    return tuple(
        pltpu.with_memory_space_constraint(v.reshape(-1), pltpu.HBM) for v in (ci, wi)
    )


def mixed_kernel(n_exc, cidx_hbm, widx_hbm, w_ref, mix_ref, *rest):
    count = N_GRP * NS
    parts = rest[:count]
    o_ref, table, cidx, widx, idx_sem = rest[count:]
    chunks = len(BOUNDS) - 1

    def index_copies(k):
        at = pl.ds(BOUNDS[k] * LANES, (BOUNDS[k + 1] - BOUNDS[k]) * LANES)
        return (
            pltpu.make_async_copy(cidx_hbm.at[at], cidx.at[at], idx_sem.at[0, k]),
            pltpu.make_async_copy(widx_hbm.at[at], widx.at[at], idx_sem.at[1, k]),
        )

    for k in range(chunks):
        for copy in index_copies(k):
            copy.start()
    for i, part in enumerate(parts):
        table[pl.ds(i * PART, PART), :] = part[...]
    size = (NQ - 1) * RA + 1

    for k in range(chunks):
        for copy in index_copies(k):
            copy.wait()

        def block(q, carry, k=k):
            start = q * RA
            for a in range(RA):
                rows = pl.ds(q * (NT * RA) + a, NT, stride=RA)
                acc = None if k == 0 else o_ref[rows, :]
                for e in range(BOUNDS[k], min(BOUNDS[k + 1], n_exc)):
                    base = e * LANES + a
                    ci = cidx.at[pl.ds(base, size)][start]
                    wi = widx.at[pl.ds(base, size)][start]
                    term = (
                        table[pl.ds(ci, NT, stride=RA), :]
                        * w_ref[pl.ds(wi, NT, stride=RA), :]
                    )
                    acc = term if acc is None else acc + term
                o_ref[rows, :] = acc
            if k == 1:
                mix = mix_ref[q, NT][:, : N_GRP * RA]
                for t in range(NT):
                    at = q * (NT * RA) + t * RA
                    stacked = [
                        table[pl.ds(pl.multiple_of(at + h * PART, RA), RA), :]
                        for h in range(N_GRP)
                    ]
                    alpha = jnp.dot(
                        mix,
                        jnp.concatenate(stacked, axis=0),
                        precision=HIGH,
                        preferred_element_type=jnp.float32,
                    )
                    target = pl.ds(pl.multiple_of(at, RA), RA)
                    o_ref[target, :] = o_ref[target, :] + alpha
            return carry

        lax.fori_loop(0, NQ, block, 0)


def mixed_call(cidx, widx, wtab, mix, parts, n_exc):
    count = N_GRP * NS
    index = pltpu.SMEM((EPAD * LANES,), jnp.int32)
    return pl.pallas_call(
        functools.partial(mixed_kernel, n_exc),
        out_shape=jax.ShapeDtypeStruct((PART, LANES), jnp.float32),
        in_specs=[HBM, HBM, VMEM, VMEM] + [VMEM] * count,
        out_specs=VMEM,
        scratch_shapes=[
            pltpu.VMEM((count * PART, LANES), jnp.float32),
            index,
            index,
            pltpu.SemaphoreType.DMA((2, len(BOUNDS) - 1)),
        ],
        compiler_params=pltpu.CompilerParams(vmem_limit_bytes=16 << 20),
        cost_estimate=pl.CostEstimate(
            flops=n_exc * NQ * RA * NT * LANES * 2,
            bytes_accessed=8 << 20,
            transcendentals=0,
        ),
        name="mixed",
    )(cidx, widx, wtab, mix, *parts)


def per_device(
    coeff,
    beta_blocks,
    block_list,
    alpha_blocks,
    partner_mask,
    exc_source,
    exc_pair,
    exc_parity,
    occupation,
    coulomb,
):
    g = lax.axis_index("grp")
    xl = lax.axis_index("xl")
    c = lax.axis_index("c")
    alpha_rows, beta_width = coeff.shape
    n_exc = exc_source.shape[0]
    n_pair = coulomb.shape[0]

    def shift(value, k):
        return lax.ppermute(
            value, "grp", [(i, (i - k) % N_GRP) for i in range(N_GRP)]
        )

    def swap(value, axis):
        return lax.ppermute(value, axis, [(0, 1), (1, 0)])

    packed = pack(g.reshape(1), partner_mask, coeff, alpha_blocks)
    arrived = lax.all_to_all(
        packed, ("z", "xh"), split_axis=0, concat_axis=0, tiled=True
    )

    sel = xl * NC + c
    place = jnp.stack([g, sel]).astype(jnp.int32)
    cidx, widx = prep_call(place, exc_source, exc_pair, exc_parity, n_pair)
    pieces = [
        lax.ppermute(occupation, ("xl", "c"), [(i, i ^ k) for i in range(NS)])
        for k in range(1, NS)
    ]
    pieces = jnp.stack([occupation] + pieces)
    ordered = [
        lax.dynamic_index_in_dim(pieces, sel ^ k, 0, keepdims=False) for k in range(NS)
    ]
    occ = jnp.concatenate(ordered, axis=1).astype(jnp.float32)
    weights = jnp.dot(coulomb, occ, precision=HIGH, preferred_element_type=jnp.float32)
    signed = jnp.concatenate([weights, -weights], axis=0)
    wtab = (
        signed.reshape(2 * n_pair // RA, RA, NT, LANES)
        .transpose(0, 2, 1, 3)
        .reshape(2 * n_pair * NT, LANES)
    )

    block_size = beta_blocks.shape[1]
    block_count = beta_width // block_size
    blocked = coeff.reshape(alpha_rows, block_count, block_size)
    block_ids = jnp.arange(block_count, dtype=jnp.int32)
    choosing = (block_list[0][:, None] == block_ids[None, :]).astype(jnp.float32)
    picked = jnp.einsum("rnk,pn->rpk", blocked, choosing, precision=HIGH)
    arrived, wtab, cidx, widx, picked = lax.optimization_barrier(
        (arrived, wtab, cidx, widx, picked)
    )
    own = arrived[:, :NT].reshape(PART, LANES)
    after, before = shift(own, 1), shift(own, N_GRP - 1)
    over = swap(own, "xl")
    again, over, after, before = lax.optimization_barrier((own, over, after, before))
    over_after, over_before = swap(after, "xl"), swap(before, "xl")
    two, over_two = shift(again, 2), shift(over, 2)
    (start, after, before, over), over_after = lax.optimization_barrier(
        ((again, after, before, over), over_after)
    )
    near = [start, after, two, before]
    across = [over, over_after, over_two, over_before]
    parts = (
        near
        + [swap(v, "c") for v in near]
        + across
        + [swap(v, "c") for v in across]
    )
    mixed_local = mixed_call(
        cidx,
        widx,
        wtab,
        arrived,
        parts,
        n_exc,
    )
    mixed = lax.all_to_all(
        mixed_local.reshape(NQ, NT, RA, LANES),
        ("z", "xh"),
        split_axis=0,
        concat_axis=0,
        tiled=True,
    )
    mixed = (
        mixed.reshape(NQ * NT, RA, LANES).transpose(1, 0, 2).reshape(alpha_rows, -1)
    )

    applied = jnp.einsum("rpk,pkl->rpl", picked, beta_blocks, precision=HIGH)
    placing = (block_list[1][:, None] == block_ids[None, :]).astype(jnp.float32)
    same_beta = jnp.einsum("rpl,pn->rnl", applied, placing, precision=HIGH).reshape(
        alpha_rows, beta_width
    )

    return mixed + same_beta


def solution(mesh):
    wide = ("z", "xh", "xl", "c")
    fine = Mesh(mesh.devices.reshape(N_GRP, NZ, NXH, NXL, NC), ("grp",) + wide)
    every = ("grp",) + wide
    in_specs = (
        P(every, None),
        P(),
        P(),
        P(every, None, None, None),
        P(every, None),
        P(None, "grp"),
        P(None, "grp"),
        P(None, "grp"),
        P(None, wide),
        P(),
    )
    return jax.shard_map(
        per_device,
        mesh=fine,
        in_specs=in_specs,
        out_specs=P(every, None),
        check_vma=False,
    )
```

```python
import functools

import jax
import jax.numpy as jnp
from jax import lax
from jax.experimental import pallas as pl
from jax.experimental.pallas import tpu as pltpu
from jax.sharding import Mesh
from jax.sharding import PartitionSpec as P

HIGH = lax.Precision.HIGHEST
RA = 8
LANES = 128
N_GRP = 4
NZ, NXH, NXL, NC = 8, 2, 2, 2
NQ = NZ * NXH
NS = NXL * NC
NT = 3
PART = NQ * NT * RA
EPAD = 96
BOUNDS = (0, 8, 48, EPAD)

SMEM = pl.BlockSpec(memory_space=pltpu.SMEM)
VMEM = pl.BlockSpec(memory_space=pltpu.VMEM)
HBM = pl.BlockSpec(memory_space=pltpu.HBM)


def pack_kernel(g_ref, mask_ref, x_ref, alpha_ref, o_ref):
    pieces = []
    for rel in range(N_GRP):
        h = (g_ref[0] + rel) & (N_GRP - 1)
        pieces.append(alpha_ref[0, h] * mask_ref[0, h].astype(jnp.float32))
    pieces.append(jnp.zeros((RA, LANES - N_GRP * RA), jnp.float32))
    coupling = jnp.concatenate(pieces, axis=1)
    for j in range(NQ):
        for t in range(NT):
            lo = (j * NT + t) * LANES
            o_ref[j, t] = x_ref[:, lo : lo + LANES]
        o_ref[j, NT] = coupling


def pack(group, mask, coeff, alpha_blocks):
    return pl.pallas_call(
        pack_kernel,
        out_shape=jax.ShapeDtypeStruct((NQ, NT + 1, RA, LANES), jnp.float32),
        in_specs=[SMEM, SMEM, VMEM, VMEM],
        out_specs=VMEM,
        name="pack",
    )(group, mask, coeff, alpha_blocks)


def prep_kernel(n_pair, place_ref, src_ref, pair_ref, par_ref, ci_ref, wi_ref):
    g, sel = place_ref[0], place_ref[1]
    n_exc, row_count = src_ref.shape
    row = lax.broadcasted_iota(jnp.int32, (LANES, row_count), 0)
    col = lax.broadcasted_iota(jnp.int32, (LANES, row_count), 1)
    want = (row >> 3) * (NS * RA) + sel * RA + (row & (RA - 1))
    pick = jnp.where(col == want, 1.0, 0.0)
    src = src_ref[...]
    rel_g = ((src >> 9) - g) & (N_GRP - 1)
    rel_s = ((src >> 3) & (NS - 1)) ^ sel
    pos = (rel_s * N_GRP + rel_g) * NQ + ((src >> 5) & (NQ - 1))
    pair = pair_ref[...] + n_pair * par_ref[...]
    for value, out in (
        (pos * (NT * RA) + (src & (RA - 1)), ci_ref),
        ((pair >> 3) * (NT * RA) + (pair & (RA - 1)), wi_ref),
    ):
        chosen = lax.dot_general(
            value.astype(jnp.float32),
            pick,
            (((1,), (1,)), ((), ())),
            precision=HIGH,
            preferred_element_type=jnp.float32,
        )
        out[pl.ds(0, n_exc), :] = (chosen + 0.5).astype(jnp.int32)
        out[pl.ds(n_exc, EPAD - n_exc), :] = jnp.zeros((EPAD - n_exc, LANES), jnp.int32)


def prep_call(place, src, pair, par, n_pair):
    shape = jax.ShapeDtypeStruct((EPAD, LANES), jnp.int32)
    ci, wi = pl.pallas_call(
        functools.partial(prep_kernel, n_pair),
        out_shape=(shape, shape),
        in_specs=[SMEM, VMEM, VMEM, VMEM],
        out_specs=(VMEM, VMEM),
        name="prep",
    )(place, src, pair, par)
    return tuple(
        pltpu.with_memory_space_constraint(v.reshape(-1), pltpu.HBM) for v in (ci, wi)
    )


def mixed_kernel(n_exc, cidx_hbm, widx_hbm, w_ref, mix_ref, *rest):
    count = N_GRP * NS
    parts = rest[:count]
    o_ref, table, cidx, widx, idx_sem = rest[count:]
    chunks = len(BOUNDS) - 1

    def index_copies(k):
        at = pl.ds(BOUNDS[k] * LANES, (BOUNDS[k + 1] - BOUNDS[k]) * LANES)
        return (
            pltpu.make_async_copy(cidx_hbm.at[at], cidx.at[at], idx_sem.at[0, k]),
            pltpu.make_async_copy(widx_hbm.at[at], widx.at[at], idx_sem.at[1, k]),
        )

    for k in range(chunks):
        for copy in index_copies(k):
            copy.start()
    for i, part in enumerate(parts):
        table[pl.ds(i * PART, PART), :] = part[...]
    size = (NQ - 1) * RA + 1

    for k in range(chunks):
        for copy in index_copies(k):
            copy.wait()

        def block(q, carry, k=k):
            start = q * RA
            for a in range(RA):
                rows = pl.ds(q * (NT * RA) + a, NT, stride=RA)
                acc = None if k == 0 else o_ref[rows, :]
                for e in range(BOUNDS[k], min(BOUNDS[k + 1], n_exc)):
                    base = e * LANES + a
                    ci = cidx.at[pl.ds(base, size)][start]
                    wi = widx.at[pl.ds(base, size)][start]
                    term = (
                        table[pl.ds(ci, NT, stride=RA), :]
                        * w_ref[pl.ds(wi, NT, stride=RA), :]
                    )
                    acc = term if acc is None else acc + term
                o_ref[rows, :] = acc
            if k == 1:
                mix = mix_ref[q, NT][:, : N_GRP * RA]
                for t in range(NT):
                    at = q * (NT * RA) + t * RA
                    stacked = [
                        table[pl.ds(pl.multiple_of(at + h * PART, RA), RA), :]
                        for h in range(N_GRP)
                    ]
                    alpha = jnp.dot(
                        mix,
                        jnp.concatenate(stacked, axis=0),
                        precision=HIGH,
                        preferred_element_type=jnp.float32,
                    )
                    target = pl.ds(pl.multiple_of(at, RA), RA)
                    o_ref[target, :] = o_ref[target, :] + alpha
            return carry

        lax.fori_loop(0, NQ, block, 0)


def mixed_call(cidx, widx, wtab, mix, parts, n_exc):
    count = N_GRP * NS
    index = pltpu.SMEM((EPAD * LANES,), jnp.int32)
    return pl.pallas_call(
        functools.partial(mixed_kernel, n_exc),
        out_shape=jax.ShapeDtypeStruct((PART, LANES), jnp.float32),
        in_specs=[HBM, HBM, VMEM, VMEM] + [VMEM] * count,
        out_specs=VMEM,
        scratch_shapes=[
            pltpu.VMEM((count * PART, LANES), jnp.float32),
            index,
            index,
            pltpu.SemaphoreType.DMA((2, len(BOUNDS) - 1)),
        ],
        compiler_params=pltpu.CompilerParams(vmem_limit_bytes=16 << 20),
        cost_estimate=pl.CostEstimate(
            flops=n_exc * NQ * RA * NT * LANES * 2,
            bytes_accessed=8 << 20,
            transcendentals=0,
        ),
        name="mixed",
    )(cidx, widx, wtab, mix, *parts)


def per_device(
    coeff,
    beta_blocks,
    block_list,
    alpha_blocks,
    partner_mask,
    exc_source,
    exc_pair,
    exc_parity,
    occupation,
    coulomb,
):
    g = lax.axis_index("grp")
    xl = lax.axis_index("xl")
    c = lax.axis_index("c")
    alpha_rows, beta_width = coeff.shape
    n_exc = exc_source.shape[0]
    n_pair = coulomb.shape[0]

    def shift(value, k):
        return lax.ppermute(
            value, "grp", [(i, (i - k) % N_GRP) for i in range(N_GRP)]
        )

    def swap(value, axis):
        return lax.ppermute(value, axis, [(0, 1), (1, 0)])

    packed = pack(g.reshape(1), partner_mask, coeff, alpha_blocks)
    arrived = lax.all_to_all(
        packed, ("z", "xh"), split_axis=0, concat_axis=0, tiled=True
    )

    sel = xl * NC + c
    place = jnp.stack([g, sel]).astype(jnp.int32)
    cidx, widx = prep_call(place, exc_source, exc_pair, exc_parity, n_pair)
    pieces = [
        lax.ppermute(occupation, ("xl", "c"), [(i, i ^ k) for i in range(NS)])
        for k in range(1, NS)
    ]
    pieces = jnp.stack([occupation] + pieces)
    ordered = [
        lax.dynamic_index_in_dim(pieces, sel ^ k, 0, keepdims=False) for k in range(NS)
    ]
    occ = jnp.concatenate(ordered, axis=1).astype(jnp.float32)
    weights = jnp.dot(coulomb, occ, precision=HIGH, preferred_element_type=jnp.float32)
    signed = jnp.concatenate([weights, -weights], axis=0)
    wtab = (
        signed.reshape(2 * n_pair // RA, RA, NT, LANES)
        .transpose(0, 2, 1, 3)
        .reshape(2 * n_pair * NT, LANES)
    )

    block_size = beta_blocks.shape[1]
    block_count = beta_width // block_size
    blocked = coeff.reshape(alpha_rows, block_count, block_size)
    block_ids = jnp.arange(block_count, dtype=jnp.int32)
    choosing = (block_list[0][:, None] == block_ids[None, :]).astype(jnp.float32)
    picked = jnp.einsum("rnk,pn->rpk", blocked, choosing, precision=HIGH)
    arrived, wtab, cidx, widx, picked = lax.optimization_barrier(
        (arrived, wtab, cidx, widx, picked)
    )
    own = arrived[:, :NT].reshape(PART, LANES)
    after, before = shift(own, 1), shift(own, N_GRP - 1)
    over = swap(own, "xl")
    again, over, after, before = lax.optimization_barrier((own, over, after, before))
    over_after, over_before = swap(after, "xl"), swap(before, "xl")
    two, over_two = shift(after, 1), shift(over, 2)
    (start, after, before, over), over_after = lax.optimization_barrier(
        ((again, after, before, over), over_after)
    )
    near = [start, after, two, before]
    across = [over, over_after, over_two, over_before]
    parts = (
        near
        + [swap(v, "c") for v in near]
        + across
        + [swap(v, "c") for v in across]
    )
    mixed_local = mixed_call(
        cidx,
        widx,
        wtab,
        arrived,
        parts,
        n_exc,
    )
    mixed = lax.all_to_all(
        mixed_local.reshape(NQ, NT, RA, LANES),
        ("z", "xh"),
        split_axis=0,
        concat_axis=0,
        tiled=True,
    )
    mixed = (
        mixed.reshape(NQ * NT, RA, LANES).transpose(1, 0, 2).reshape(alpha_rows, -1)
    )

    applied = jnp.einsum("rpk,pkl->rpl", picked, beta_blocks, precision=HIGH)
    placing = (block_list[1][:, None] == block_ids[None, :]).astype(jnp.float32)
    same_beta = jnp.einsum("rpl,pn->rnl", applied, placing, precision=HIGH).reshape(
        alpha_rows, beta_width
    )

    return mixed + same_beta


def solution(mesh):
    wide = ("z", "xh", "xl", "c")
    fine = Mesh(mesh.devices.reshape(N_GRP, NZ, NXH, NXL, NC), ("grp",) + wide)
    every = ("grp",) + wide
    in_specs = (
        P(every, None),
        P(),
        P(),
        P(every, None, None, None),
        P(every, None),
        P(None, "grp"),
        P(None, "grp"),
        P(None, "grp"),
        P(None, wide),
        P(),
    )
    return jax.shard_map(
        per_device,
        mesh=fine,
        in_specs=in_specs,
        out_specs=P(every, None),
        check_vma=False,
    )
```
